256 devices in a mesh: dp: 16 (over z_hi, x, core), tp: 4 (over z_lo), section: 4 (over y).
Axes of the slice: x: 4, y: 4, z: 8 (z_hi: 2, z_lo: 4; z = z_hi * 4 + z_lo), core: 2. Of those that a mesh axis runs over, the one named last changes fastest.
Arguments:
- tokens: bfloat16 [2048, 2304], P('dp', 'section'), may hold values from -6 to 6
- hidden_grad: bfloat16 [2048, 18432], P('dp', ('tp', 'section')), may hold values from -6 to 6
- norm_gain: float32 [2304], replicated, may hold values from 0.5 to 1.5
- w_gate: bfloat16 [2304, 18432], P('dp', ('tp', 'section')), may hold values from -0.125 to 0.125
- w_up: bfloat16 [2304, 18432], P('dp', ('tp', 'section')), may hold values from -0.125 to 0.125
Outputs:
- grad_tokens: bfloat16 [2048, 2304], P('dp', ('tp', 'section'))
- grad_gain: float32 [2304], P(('tp', 'section'))
- grad_gate: bfloat16 [2304, 18432], P('dp', ('tp', 'section'))
- grad_up: bfloat16 [2304, 18432], P('dp', ('tp', 'section'))
The draws below stay inside these ranges and needn't reach their ends.
All inputs are finite; a program needn't handle non-finite values.
Results may differ from the reference program's by a relative error of at most 0.018.
Values may be sent and summed in bfloat16 or wider, within the bound.
No kernel may reach another device: no remote copies, remote signals or barrier semaphores. Data moves between devices by JAX's collectives and lax.ppermute only.
A program may use at most 128 MiB of HBM per device.

```python
import jax
import jax.numpy as jnp
from jax import lax

D = 2304
FF = 18432
TOK_DEV = 128
TOKENS = 2048
N_DP = 16
N_TP = 4
N_SECTION = 4


def level_of(own_key, extent, cuts, smallest, top_value):
    gain, own = 1.0, jax.random.fold_in(own_key, 6)
    for position, shards_of in cuts:
        heights = jnp.exp(jax.random.uniform(jax.random.fold_in(own, position), (shards_of,), jnp.float32, smallest / len(cuts), top_value / len(cuts)))
        gain = gain * jnp.repeat(heights, extent[position] // shards_of).reshape([-1 if axis == position else 1 for axis in range(len(extent))])
    return gain


def centred(key, dims, deviation, bound, cuts=(), held_as=jnp.bfloat16):
    drawn = jax.random.normal(key, dims, jnp.float32) * deviation
    if len(cuts) > 0:
        drawn = level_of(key, dims, cuts, -0.22, 0.18) * drawn
    return jnp.clip(drawn, min=-bound, max=bound).astype(held_as)


def setup_inputs(seed: int = 0) -> dict:
    key_list = jax.random.split(jax.random.key(seed), 6)
    return {
        "tokens": centred(key_list[0], (TOKENS, D), 1.0, 6.0, ((0, 16), (1, 4))),
        "hidden_grad": centred(key_list[1], (TOKENS, FF), 1.0, 6.0, ((0, 16), (1, 16))),
        "norm_gain": jnp.clip(1.0 + 0.1 * jax.random.normal(key_list[2], (D,), jnp.float32), 0.5, 1.5),
        "w_gate": centred(key_list[3], (D, FF), D ** -0.5, 0.125, ((0, 16), (1, 16))),
        "w_up": centred(key_list[4], (D, FF), D ** -0.5, 0.125, ((0, 16), (1, 16))),
    }


epsilon = 1e-06

def gated_unit(gate, up):
    return jax.nn.gelu(gate, approximate=True) * up

def rounded(value):
    return lax.optimization_barrier(value.astype(jnp.bfloat16)).astype(jnp.float32)

def reference(tokens, hidden_grad, norm_gain, w_gate, w_up):
    groups = N_TP * N_SECTION
    fwidth = FF // groups
    gate_blocks = w_gate.astype(jnp.float32).reshape(D, groups, fwidth)
    up_blocks = w_up.astype(jnp.float32).reshape(D, groups, fwidth)

    def one_group(index, carry):
        sum_gate, sum_up, gain_total, result = carry
        start = (index * TOK_DEV).astype(jnp.int32)
        rows_in = lax.dynamic_slice_in_dim(tokens, start, TOK_DEV, 0)
        back = lax.dynamic_slice_in_dim(hidden_grad, start, TOK_DEV, 0).astype(jnp.float32)
        inputs = rows_in.astype(jnp.float32)
        inv_rms = lax.rsqrt(lax.optimization_barrier(jnp.mean(inputs * inputs, axis=1)) + epsilon)
        normed = (inputs * inv_rms[:, None] * norm_gain).astype(jnp.bfloat16)
        gate = jnp.dot(normed, w_gate, preferred_element_type=jnp.float32)
        up = jnp.dot(normed, w_up, preferred_element_type=jnp.float32)
        hidden, pull = jax.vjp(gated_unit, gate, up)
        d_gate, d_up = pull(back)
        d_gate = d_gate.astype(jnp.bfloat16)
        d_up = d_up.astype(jnp.bfloat16)
        gate_split = d_gate.astype(jnp.float32).reshape(TOK_DEV, groups, fwidth)
        up_split = d_up.astype(jnp.float32).reshape(TOK_DEV, groups, fwidth)
        parts = jnp.einsum('rbf,dbf->bdr', gate_split, gate_blocks) + jnp.einsum('rbf,dbf->bdr', up_split, up_blocks)
        d_normed = lax.optimization_barrier(jnp.sum(rounded(parts), axis=0)).T
        gain_total = gain_total + lax.optimization_barrier(jnp.sum(d_normed * inputs * inv_rms[:, None], axis=0))
        row_sum = lax.optimization_barrier(jnp.sum(inputs * norm_gain * d_normed, axis=1))
        grad_rows = inv_rms[:, None] * norm_gain * d_normed - inputs * (inv_rms ** 3 * row_sum / D)[:, None]
        result = lax.dynamic_update_slice(result, grad_rows.astype(jnp.bfloat16), (start, jnp.zeros((), jnp.int32)))
        sum_gate = sum_gate + rounded(jnp.dot(normed.T, d_gate, preferred_element_type=jnp.float32))
        sum_up = sum_up + rounded(jnp.dot(normed.T, d_up, preferred_element_type=jnp.float32))
        return (sum_gate, sum_up, gain_total, result)
    empty = jnp.zeros((D, FF), jnp.float32)
    start_carry = (empty, empty, jnp.zeros((D,), jnp.float32), jnp.zeros((TOKENS, D), jnp.bfloat16))
    sum_gate, sum_up, gain_total, result = lax.fori_loop(0, N_DP, one_group, start_carry)
    return (result, gain_total, sum_gate.astype(jnp.bfloat16), sum_up.astype(jnp.bfloat16))
```

```python
import jax
import jax.numpy as jnp
from jax import lax
from jax.sharding import Mesh
from jax.sharding import PartitionSpec as P

DP = ("zh", "x", "core")
COLS = ("tp", "sec")
EPS = 1e-06
LANES = 128
F32 = jnp.float32
BF16 = jnp.bfloat16


def turned(array, axis, by):
    n = lax.axis_size(axis)
    return lax.ppermute(array, axis, [(i, (i + by) % n) for i in range(n)])


def swapped(array, axis):
    return turned(array, axis, 1)


def crossed(array):
    pairs = [(i, 3 - i) for i in range(4)]
    return lax.ppermute(array, ("zh", "core"), pairs)


def at(array, index):
    return lax.dynamic_index_in_dim(array, index, 0, keepdims=False)


def parts_of(width):
    main = width // LANES // 4 * LANES
    rest = width // 4 - main
    return main, rest


def column_blocks(arrays):
    main, rest = parts_of(arrays[0].shape[1])
    blocks = []
    for q in range(4):
        wide = [a[:, q * main : (q + 1) * main] for a in arrays]
        thin = [a[:, 4 * main + q * rest : 4 * main + (q + 1) * rest] for a in arrays]
        blocks.append(jnp.concatenate(wide + thin, axis=1))
    return jnp.stack(blocks)


def split_pair(block):
    main, rest = parts_of(block.shape[1] * 2)
    first = jnp.concatenate([block[:, :main], block[:, 2 * main : 2 * main + rest]], axis=1)
    second = jnp.concatenate([block[:, main : 2 * main], block[:, 2 * main + rest :]], axis=1)
    return first, second


def join_pair(first, second):
    main, rest = parts_of(first.shape[1] * 4)
    return jnp.concatenate(
        [first[:, :main], second[:, :main], first[:, main:], second[:, main:]], axis=1
    )


def ordered(own, other, index):
    return jnp.where(index == 0, jnp.stack([own, other]), jnp.stack([other, own]))


def ring_gather(block, axis):
    left = turned(block, axis, 1)
    right = turned(block, axis, -1)
    far_a = turned(left[0], axis, 1)
    far_b = turned(right[1], axis, -1)
    return block, left, right, jnp.stack([far_a, far_b])


def ring_scatter(part, axis):
    far = part(2).astype(BF16)
    got_a = turned(far[0], axis, 1)
    got_b = turned(far[1], axis, -1)
    ahead, behind = part(1), part(-1)
    ahead = jnp.stack([ahead[0] + got_a.astype(F32), ahead[1]]).astype(BF16)
    behind = jnp.stack([behind[0], behind[1] + got_b.astype(F32)]).astype(BF16)
    got_ahead = turned(ahead, axis, 1)
    got_behind = turned(behind, axis, -1)
    return part(0) + got_ahead.astype(F32) + got_behind.astype(F32)


def derivatives(gate, up, back):
    hidden, pull = jax.vjp(lambda g, u: jax.nn.gelu(g, approximate=True) * u, gate, up)
    return pull(back)


def shards(tokens, hidden_grad, norm_gain, w_gate, w_up):
    rows, width = w_gate.shape
    group = tokens.shape[0]
    features = norm_gain.shape[0]
    zh, x, core = (lax.axis_index(a) for a in DP)
    tp, sec = (lax.axis_index(a) for a in COLS)

    w_blocks = column_blocks((w_gate, w_up)).reshape(2, 2, rows, -1)
    w_near, w_away = at(w_blocks, zh), at(w_blocks, 1 - zh)
    away_same = swapped(at(w_away, core), "zh")
    away_cross = crossed(at(w_away, 1 - core))
    near_cross = swapped(at(w_near, 1 - core), "core")
    near = ordered(at(w_near, core), near_cross, core)
    away = ordered(away_same, away_cross, core)

    h_blocks = column_blocks((hidden_grad,)).reshape(2, 2, group, -1)
    h_near, h_away = at(h_blocks, zh), at(h_blocks, 1 - zh)
    back = jnp.concatenate(
        [
            at(h_near, core),
            swapped(at(h_away, core), "zh"),
            swapped(at(h_near, 1 - core), "core"),
            crossed(at(h_away, 1 - core)),
        ],
        axis=0,
    )

    own_t = tokens.T
    both = jnp.concatenate([own_t, swapped(own_t, "zh")], axis=1)
    left = turned(both, "sec", 1)
    right = turned(both, "sec", -1)
    half = both.shape[0] // 2
    far = jnp.concatenate(
        [turned(left[:half], "sec", 1), turned(right[half:], "sec", -1)], axis=0
    )
    inputs = jnp.zeros((4, *both.shape), BF16)
    for by, piece in ((0, both), (-1, left), (1, right), (2, far)):
        inputs = lax.dynamic_update_index_in_dim(inputs, piece, (sec + by) % 4, 0)
    inputs = inputs.reshape(features, 2 * group)
    wide = inputs.astype(F32)
    inv_rms = lax.rsqrt(jnp.mean(wide * wide, axis=0) + EPS)
    normed = (wide * inv_rms * norm_gain[:, None]).astype(BF16)
    normed = jnp.concatenate([normed, swapped(normed, "core")], axis=1)

    full = jnp.zeros((2, 4, 2, rows, w_blocks.shape[-1]), BF16)
    for place, pair in ((zh, near), (1 - zh, away)):
        own, left, right, far = ring_gather(pair, "x")
        for by, piece in ((0, own), (-1, left), (1, right), (2, far)):
            full = lax.dynamic_update_slice(
                full, piece[None, None], (place, (x + by) % 4, 0, 0, 0)
            )
    full = full.reshape(features, -1)

    product = lax.dot_general(
        normed, full, (((0,), (0,)), ((), ())), preferred_element_type=F32
    )
    gate, up = split_pair(product)
    d_gate, d_up = derivatives(gate, up, back.astype(F32))
    d_gate, d_up = d_gate.astype(BF16), d_up.astype(BF16)
    row_part = jnp.sum(d_gate.astype(F32) * gate + d_up.astype(F32) * up, axis=1)
    d_both = join_pair(d_gate, d_up)

    d_normed = lax.dot_general(
        full, d_both, (((1,), (1,)), ((), ())), preferred_element_type=F32
    )
    mine, theirs = d_normed[:, : 2 * group], d_normed[:, 2 * group :].astype(BF16)
    mine = mine + swapped(theirs, "core").astype(F32)
    by_owner = mine.reshape(4, 4, features // 16, 2 * group)

    def for_section(by):
        block = lax.dynamic_index_in_dim(by_owner, (sec + by) % 4, 1, keepdims=False)
        return block.reshape(2, 2, features // 16, 2 * group)

    mine = ring_scatter(for_section, "sec").reshape(4, features // 16, 2 * group)
    total = at(mine, tp)
    for by in (1, 2, 3):
        total = total + turned(at(mine, (tp + by) % 4).astype(BF16), "tp", by).astype(F32)
    d_own = total[:, :group] + swapped(total[:, group:].astype(BF16), "zh").astype(F32)

    row_part = row_part.reshape(4, group)
    row_part = row_part[:2] + swapped(row_part[2:], "core")
    row_part = row_part[0] + swapped(row_part[1], "zh")
    for axis in COLS:
        row_part = row_part + sum(turned(row_part, axis, by) for by in (1, 2, 3))

    own_rows = features // 16
    offset = (tp * 4 + sec) * own_rows
    own_inputs = lax.dynamic_slice(inputs, (offset, 0), (own_rows, group)).astype(F32)
    own_gain = lax.dynamic_slice_in_dim(norm_gain, offset, own_rows, 0)[:, None]
    inv = inv_rms[:group]
    grad_gain = jnp.sum(d_own * own_inputs * inv, axis=1)
    grad_tokens = inv * own_gain * d_own - own_inputs * (inv**2 * row_part / features)
    for axis in ("core", "zh"):
        grad_gain = grad_gain + swapped(grad_gain, axis)
    grad_gain = grad_gain + sum(turned(grad_gain, "x", by) for by in (1, 2, 3))

    by_rows = normed.reshape(2, 4, 2 * rows, 4 * group)

    def summed(place):
        def part(by):
            mine = lax.dynamic_slice(
                by_rows, (place, (x + by) % 4, 0, 0), (1, 1, 2 * rows, 4 * group)
            )
            out = jnp.dot(mine[0, 0], d_both, preferred_element_type=F32)
            return out.reshape(2, rows, -1)

        return ring_scatter(part, "x").astype(BF16)

    g_away = summed(1 - zh)
    g_near = summed(zh)
    got_same = swapped(at(g_away, core), "zh")
    got_cross = crossed(at(g_away, 1 - core))
    got_core = swapped(at(g_near, 1 - core), "core")
    near = ordered(at(g_near, core), got_core, core)
    away = ordered(got_same, got_cross, core)
    blocks = ordered(near, away, zh).reshape(4, rows, -1)
    main, rest = parts_of(width)

    def joined(wide_from, thin_from):
        wide = [blocks[q, :, wide_from : wide_from + main] for q in range(4)]
        thin = [blocks[q, :, thin_from : thin_from + rest] for q in range(4)]
        return jnp.concatenate(wide + thin, axis=1)

    grad_gate = joined(0, 2 * main)
    grad_up = joined(main, 2 * main + rest)
    return grad_tokens.T.astype(BF16), grad_gain, grad_gate, grad_up


def solution(mesh):
    split = Mesh(
        mesh.devices.reshape(2, 4, 2, mesh.shape["tp"], mesh.shape["section"]),
        (*DP, *COLS),
    )
    weights = P(DP, COLS)
    return jax.shard_map(
        shards,
        mesh=split,
        in_specs=(P(DP, "sec"), weights, P(), weights, weights),
        out_specs=(weights, P(COLS), weights, weights),
        check_vma=False,
    )
```

```python
import functools

import jax
import jax.numpy as jnp
from jax import lax
from jax.experimental import pallas as pl
from jax.experimental.pallas import tpu as pltpu
from jax.sharding import Mesh
from jax.sharding import PartitionSpec as P

DP = ("zh", "x", "core")
COLS = ("tp", "sec")
EPS = 1e-06
LANES = 128
EXTRA = 16
F32 = jnp.float32
BF16 = jnp.bfloat16
SDS = jax.ShapeDtypeStruct


def turned(array, axis, by):
    n = lax.axis_size(axis)
    return lax.ppermute(array, axis, [(i, (i + by) % n) for i in range(n)])


def swapped(array, axis):
    return turned(array, axis, 1)


def at(array, index):
    return lax.dynamic_index_in_dim(array, index, 0, keepdims=False)


def parts_of(width):
    main = width // LANES // 4 * LANES
    rest = width // 4 - main
    return main, rest


def pack_kernel(main, rest, rows, place, gate_ref, up_ref, back_ref, own_ref, other_ref, away_ref):
    half = back_ref.shape[0] // 2
    sources = (
        (0, rows, gate_ref, up_ref),
        (rows, half, back_ref.at[pl.ds(0, half)], back_ref.at[pl.ds(half, half)]),
    )
    for r in range(4):
        q = (place[0] ^ (r // 2)) * 2 + (place[1] ^ (r % 2))
        out = (own_ref, other_ref, away_ref.at[0], away_ref.at[1])[r]
        wide = pl.ds(pl.multiple_of(q * main, LANES), main)
        for start, count, first, second in sources:
            here = pl.ds(start, count)
            out[here, pl.ds(0, main)] = first[:, wide]
            out[here, pl.ds(main, main)] = second[:, wide]
            thin = []
            for ref in (first, second):
                tail = ref[:, pl.ds(4 * main, 4 * rest)]
                pick = tail[:, :rest]
                for k in range(1, 4):
                    pick = jnp.where(q == k, tail[:, k * rest : (k + 1) * rest], pick)
                thin.append(pick)
            out[here, pl.ds(2 * main, 2 * rest)] = jnp.concatenate(thin, axis=1)


def packed(place, w_gate, w_up, hidden_grad):
    rows, width = w_gate.shape
    main, rest = parts_of(width)
    height = rows + hidden_grad.shape[0] // 2
    block = SDS((height, width // 2), BF16)
    return pl.pallas_call(
        functools.partial(pack_kernel, main, rest, rows),
        out_shape=(block, block, SDS((2, *block.shape), BF16)),
        in_specs=[pl.BlockSpec(memory_space=pltpu.SMEM)]
        + [pl.BlockSpec(memory_space=pltpu.VMEM)] * 3,
        out_specs=(pl.BlockSpec(memory_space=pltpu.VMEM),) * 3,
        name="pack",
    )(place, w_gate, w_up, hidden_grad)


def split_pair(block):
    main, rest = parts_of(block.shape[1] * 2)
    first = jnp.concatenate([block[:, :main], block[:, 2 * main : 2 * main + rest]], axis=1)
    second = jnp.concatenate([block[:, main : 2 * main], block[:, 2 * main + rest :]], axis=1)
    return first, second


def join_pair(first, second):
    main, rest = parts_of(first.shape[1] * 4)
    return jnp.concatenate(
        [first[:, :main], second[:, :main], first[:, main:], second[:, main:]], axis=1
    )


def ordered(own, other, index):
    return jnp.where(index == 0, jnp.stack([own, other]), jnp.stack([other, own]))


def with_rows(block, row):
    high = row.astype(BF16)
    low = (row - high.astype(F32)).astype(BF16)
    tail = jnp.concatenate(
        [high[None], low[None], jnp.zeros((EXTRA - 2, row.shape[0]), BF16)], axis=0
    )
    return jnp.concatenate([block.astype(BF16).reshape(-1, row.shape[0]), tail], axis=0)


def without_rows(packed_rows):
    n = packed_rows.shape[0] - EXTRA
    wide = packed_rows.astype(F32)
    return wide[:n], wide[n] + wide[n + 1]


def derivatives(gate, up, back):
    hidden, pull = jax.vjp(lambda g, u: jax.nn.gelu(g, approximate=True) * u, gate, up)
    return pull(back)


def shards(tokens, hidden_grad, norm_gain, w_gate, w_up):
    rows, width = w_gate.shape
    group = tokens.shape[0]
    features = norm_gain.shape[0]
    zh, x, core = (lax.axis_index(a) for a in DP)
    tp, sec = (lax.axis_index(a) for a in COLS)

    own_t = tokens.T
    both = jnp.concatenate([own_t, swapped(own_t, "zh")], axis=1)

    place = jnp.stack([zh, core]).astype(jnp.int32)
    near_own, near_other, away = packed(place, w_gate, w_up, hidden_grad)
    away = swapped(away, "zh")
    near_other = swapped(near_other, "core")
    away_own, away_other = away[0], swapped(away[1], "core")
    back = jnp.concatenate(
        [
            half
            for block in (near_own, away_own, near_other, away_other)
            for half in split_pair(block[rows:])
        ],
        axis=0,
    )

    inputs = jnp.zeros((4, *both.shape), BF16)
    inputs = lax.dynamic_update_index_in_dim(inputs, both, sec, 0)
    for by in (1, 3, 2):
        piece = turned(both, "sec", by)
        inputs = lax.dynamic_update_index_in_dim(inputs, piece, (sec - by) % 4, 0)
    inputs = inputs.reshape(features, 2 * group)
    wide = inputs.astype(F32)
    inv_rms = lax.rsqrt(jnp.mean(wide * wide, axis=0) + EPS)
    normed = (wide * inv_rms * norm_gain[:, None]).astype(BF16)
    normed = jnp.concatenate([normed, swapped(normed, "core")], axis=1)

    full = jnp.zeros((2, 4, 2, rows, width // 2), BF16)
    for zplace, own, other in (
        (zh, near_own, near_other),
        (1 - zh, away_own, away_other),
    ):
        pair = ordered(own[:rows], other[:rows], core)
        full = lax.dynamic_update_slice(full, pair[None, None], (zplace, x, 0, 0, 0))
        for by in (1, 3, 2):
            piece = turned(pair, "x", by)
            full = lax.dynamic_update_slice(
                full, piece[None, None], (zplace, (x - by) % 4, 0, 0, 0)
            )
    full = full.reshape(features, -1)

    product = lax.dot_general(
        normed, full, (((0,), (0,)), ((), ())), preferred_element_type=F32
    )
    gate, up = split_pair(product)
    d_gate, d_up = derivatives(gate, up, back.astype(F32))
    d_gate, d_up = d_gate.astype(BF16), d_up.astype(BF16)
    row_part = jnp.sum(d_gate.astype(F32) * gate + d_up.astype(F32) * up, axis=1)
    d_both = join_pair(d_gate, d_up)

    d_normed = lax.dot_general(
        full, d_both, (((1,), (1,)), ((), ())), preferred_element_type=F32
    )
    theirs = with_rows(d_normed[:, 2 * group :], row_part[2 * group :])
    got, row_got = without_rows(swapped(theirs, "core"))
    mine, row = d_normed[:, : 2 * group] + got, row_part[: 2 * group] + row_got
    own_rows = features // 16
    mine = mine.reshape(4, 4, own_rows, 2 * group)

    def section(index):
        block = lax.dynamic_index_in_dim(mine, index % 4, 1, keepdims=False)
        return block.reshape(4 * own_rows, 2 * group)

    total, row_total = section(sec), row
    for by in (2, 1, 3):
        got, row_got = without_rows(turned(with_rows(section(sec + by), row), "sec", by))
        total, row_total = total + got, row_total + row_got
    mine, row = total.reshape(4, own_rows, 2 * group), row_total
    total, row_total = at(mine, tp), row
    for by in (2, 1, 3):
        got, row_got = without_rows(turned(with_rows(at(mine, (tp + by) % 4), row), "tp", by))
        total, row_total = total + got, row_total + row_got
    got, row_got = without_rows(
        swapped(with_rows(total[:, group:], row_total[group:]), "zh")
    )
    d_own, row_sum = total[:, :group] + got, row_total[:group] + row_got

    offset = (tp * 4 + sec) * own_rows
    own_inputs = lax.dynamic_slice(inputs, (offset, 0), (own_rows, group)).astype(F32)
    own_gain = lax.dynamic_slice_in_dim(norm_gain, offset, own_rows, 0)[:, None]
    inv = inv_rms[:group]
    grad_gain = jnp.sum(d_own * own_inputs * inv, axis=1)
    grad_tokens = inv * own_gain * d_own - own_inputs * (inv**2 * row_sum / features)
    for axis in ("core", "zh"):
        grad_gain = grad_gain + swapped(grad_gain, axis)
    grad_gain = grad_gain + sum(turned(grad_gain, "x", by) for by in (1, 2, 3))

    by_rows = normed.reshape(2, 4, 2 * rows, 4 * group)

    def summed(zplace):
        def part(by):
            mine = lax.dynamic_slice(
                by_rows, (zplace, (x + by) % 4, 0, 0), (1, 1, 2 * rows, 4 * group)
            )
            return jnp.dot(mine[0, 0], d_both, preferred_element_type=F32)

        got = [turned(part(by).astype(BF16), "x", by) for by in (2, 1, 3)]
        out = part(0) + sum(g.astype(F32) for g in got)
        return out.astype(BF16).reshape(2, rows, -1)

    g_away = swapped(summed(1 - zh), "zh")
    g_near = summed(zh)
    keep = jnp.stack([at(g_near, core), at(g_away, core)])
    give = swapped(jnp.stack([at(g_near, 1 - core), at(g_away, 1 - core)]), "core")
    near = ordered(keep[0], give[0], core)
    away = ordered(keep[1], give[1], core)
    blocks = ordered(near, away, zh).reshape(4, rows, -1)
    main, rest = parts_of(width)

    def joined(wide_from, thin_from):
        wide = [blocks[q, :, wide_from : wide_from + main] for q in range(4)]
        thin = [blocks[q, :, thin_from : thin_from + rest] for q in range(4)]
        return jnp.concatenate(wide + thin, axis=1)

    grad_gate = joined(0, 2 * main)
    grad_up = joined(main, 2 * main + rest)
    return grad_tokens.T.astype(BF16), grad_gain, grad_gate, grad_up


def solution(mesh):
    split = Mesh(
        mesh.devices.reshape(2, 4, 2, mesh.shape["tp"], mesh.shape["section"]),
        (*DP, *COLS),
    )
    weights = P(DP, COLS)
    return jax.shard_map(
        shards,
        mesh=split,
        in_specs=(P(DP, "sec"), weights, P(), weights, weights),
        out_specs=(weights, P(COLS), weights, weights),
        check_vma=False,
    )
```

```python
import functools

import jax
import jax.numpy as jnp
from jax import lax
from jax.experimental import pallas as pl
from jax.experimental.pallas import tpu as pltpu
from jax.sharding import Mesh
from jax.sharding import PartitionSpec as P

DP = ("zh", "x", "core")
COLS = ("tp", "sec")
EPS = 1e-06
LANES = 128
EXTRA = 16
F32 = jnp.float32
BF16 = jnp.bfloat16
SDS = jax.ShapeDtypeStruct


def turned(array, axis, by):
    n = lax.axis_size(axis)
    return lax.ppermute(array, axis, [(i, (i + by) % n) for i in range(n)])


def swapped(array, axis):
    return turned(array, axis, 1)


def at(array, index):
    return lax.dynamic_index_in_dim(array, index, 0, keepdims=False)


def parts_of(width):
    main = width // LANES // 4 * LANES
    rest = width // 4 - main
    return main, rest


def pack_kernel(main, rest, rows, aways, gate_ref, up_ref, back_ref, *outs):
    half = back_ref.shape[0] // 2
    zh, core = lax.axis_index("zh"), lax.axis_index("core")
    sources = (
        (0, rows, gate_ref, up_ref),
        (rows, half, back_ref.at[pl.ds(0, half)], back_ref.at[pl.ds(half, half)]),
    )
    for other, out in enumerate(outs):
        q = (zh ^ aways) * 2 + (core ^ other)
        wide = pl.ds(pl.multiple_of(q * main, LANES), main)
        for start, count, first, second in sources:
            here = pl.ds(start, count)
            out[here, pl.ds(0, main)] = first[:, wide]
            out[here, pl.ds(main, main)] = second[:, wide]
            thin = []
            for ref in (first, second):
                tail = ref[:, pl.ds(4 * main, 4 * rest)]
                pick = tail[:, :rest]
                for k in range(1, 4):
                    pick = jnp.where(q == k, tail[:, k * rest : (k + 1) * rest], pick)
                thin.append(pick)
            out[here, pl.ds(2 * main, 2 * rest)] = jnp.concatenate(thin, axis=1)


def packed(aways, w_gate, w_up, hidden_grad):
    rows, width = w_gate.shape
    main, rest = parts_of(width)
    height = rows + hidden_grad.shape[0] // 2
    block = pltpu.VMEM((height, width // 2), BF16)
    return pl.pallas_call(
        functools.partial(pack_kernel, main, rest, rows, aways),
        out_shape=(block,) * 2,
        in_specs=[pl.BlockSpec(memory_space=pltpu.VMEM)] * 3,
        out_specs=(pl.BlockSpec(memory_space=pltpu.VMEM),) * 2,
        name="pack",
    )(w_gate, w_up, hidden_grad)


def join_kernel(main, rest, keep_ref, give_ref, gate_ref, up_ref):
    zh, core = lax.axis_index("zh"), lax.axis_index("core")
    tails = [[None] * 4, [None] * 4]
    for aways in range(2):
        for other, ref in enumerate((keep_ref, give_ref)):
            q = (zh ^ aways) * 2 + (core ^ other)
            wide = pl.ds(pl.multiple_of(q * main, LANES), main)
            gate_ref[:, wide] = ref[aways, :, pl.ds(0, main)]
            up_ref[:, wide] = ref[aways, :, pl.ds(main, main)]
            tail = ref[aways, :, pl.ds(2 * main, 2 * rest)]
            for i in range(2):
                thin = tail[:, i * rest : (i + 1) * rest]
                for k in range(4):
                    old = tails[i][k]
                    tails[i][k] = thin if old is None else jnp.where(q == k, thin, old)
    gate_ref[:, pl.ds(4 * main, 4 * rest)] = jnp.concatenate(tails[0], axis=1)
    up_ref[:, pl.ds(4 * main, 4 * rest)] = jnp.concatenate(tails[1], axis=1)


def joined(keep, give):
    _, rows, half = keep.shape
    main, rest = parts_of(half * 2)
    out = SDS((rows, half * 2), BF16)
    return pl.pallas_call(
        functools.partial(join_kernel, main, rest),
        out_shape=(out, out),
        in_specs=[pl.BlockSpec(memory_space=pltpu.VMEM)] * 2,
        out_specs=(pl.BlockSpec(memory_space=pltpu.VMEM),) * 2,
        name="join",
    )(keep, give)


def split_pair(block):
    main, rest = parts_of(block.shape[1] * 2)
    first = jnp.concatenate([block[:, :main], block[:, 2 * main : 2 * main + rest]], axis=1)
    second = jnp.concatenate([block[:, main : 2 * main], block[:, 2 * main + rest :]], axis=1)
    return first, second


def join_pair(first, second):
    main, rest = parts_of(first.shape[1] * 4)
    return jnp.concatenate(
        [first[:, :main], second[:, :main], first[:, main:], second[:, main:]], axis=1
    )


def ordered(own, other, index):
    return jnp.where(index == 0, jnp.stack([own, other]), jnp.stack([other, own]))


def with_rows(block, row):
    high = row.astype(BF16)
    low = (row - high.astype(F32)).astype(BF16)
    tail = jnp.concatenate(
        [high[None], low[None], jnp.zeros((EXTRA - 2, row.shape[0]), BF16)], axis=0
    )
    return jnp.concatenate([block.astype(BF16).reshape(-1, row.shape[0]), tail], axis=0)


def without_rows(packed_rows):
    n = packed_rows.shape[0] - EXTRA
    wide = packed_rows.astype(F32)
    return wide[:n], wide[n] + wide[n + 1]


def derivatives(gate, up, back):
    hidden, pull = jax.vjp(lambda g, u: jax.nn.gelu(g, approximate=True) * u, gate, up)
    return pull(back)


def shards(tokens, hidden_grad, norm_gain, w_gate, w_up):
    rows, width = w_gate.shape
    group = tokens.shape[0]
    features = norm_gain.shape[0]
    own_rows = features // 16
    zh, x, core = (lax.axis_index(a) for a in DP)
    tp, sec = (lax.axis_index(a) for a in COLS)

    own_t = tokens.T
    far_t = swapped(own_t, "zh")

    away_own, away_other = packed(1, w_gate, w_up, hidden_grad)
    near_own, near_other = packed(0, w_gate, w_up, hidden_grad)
    away_own, away_other = swapped(away_own, "zh"), swapped(away_other, "zh")
    near_other = swapped(near_other, "core")

    full = jnp.zeros((2, 4, 2, rows, width // 2), BF16)

    def placed(full, pieces, zplace, cplace):
        for by, piece in zip((0, 1, 3, 2), pieces):
            piece = piece.reshape(1, 1, -1, rows, width // 2)
            full = lax.dynamic_update_slice(full, piece, (zplace, (x - by) % 4, cplace, 0, 0))
        return full

    pair = ordered(near_own[:rows], near_other[:rows], core)
    got = [turned(pair, "x", by) for by in (1, 3, 2)]
    far_t, *got = lax.optimization_barrier((far_t, *got))
    full = placed(full, (pair, *got), zh, 0)

    both = jnp.concatenate([own_t, far_t], axis=1)
    both, away_own = lax.optimization_barrier((both, away_own))
    section_got = [turned(both, "sec", by) for by in (1, 3, 2)]
    own_got = [turned(away_own[:rows], "x", by) for by in (1, 3, 2)]

    inputs = jnp.zeros((4, *both.shape), BF16)
    for by, piece in zip((0, 1, 3, 2), (both, *section_got)):
        inputs = lax.dynamic_update_index_in_dim(inputs, piece, (sec - by) % 4, 0)
    inputs = inputs.reshape(features, 2 * group)
    wide = inputs.astype(F32)
    inv_rms = lax.rsqrt(jnp.mean(wide * wide, axis=0) + EPS)
    normed = (wide * inv_rms * norm_gain[:, None]).astype(BF16)
    normed, away_other = lax.optimization_barrier((normed, away_other))
    away_other = swapped(away_other, "core")
    normed = jnp.concatenate([normed, swapped(normed, "core")], axis=1)

    other_got = [turned(away_other[:rows], "x", by) for by in (1, 3, 2)]
    full = placed(full, (away_own[:rows], *own_got), 1 - zh, core)
    full = placed(full, (away_other[:rows], *other_got), 1 - zh, 1 - core)
    full = full.reshape(features, -1)
    back = jnp.concatenate(
        [
            half
            for block in (near_own, away_own, near_other, away_other)
            for half in split_pair(block[rows:])
        ],
        axis=0,
    )

    product = lax.dot_general(
        normed, full, (((0,), (0,)), ((), ())), preferred_element_type=F32
    )
    gate, up = split_pair(product)
    d_gate, d_up = derivatives(gate, up, back.astype(F32))
    d_gate, d_up = d_gate.astype(BF16), d_up.astype(BF16)
    row_part = jnp.sum(d_gate.astype(F32) * gate + d_up.astype(F32) * up, axis=1)
    d_both = join_pair(d_gate, d_up)

    def d_normed(d):
        return lax.dot_general(full, d, (((1,), (1,)), ((), ())), preferred_element_type=F32)

    theirs = with_rows(d_normed(d_both[2 * group :]), row_part[2 * group :])
    got, row_got = without_rows(swapped(theirs, "core"))
    mine, row = d_normed(d_both[: 2 * group]) + got, row_part[: 2 * group] + row_got
    mine = mine.reshape(4, 4, own_rows, 2 * group)

    by_rows = normed.reshape(2, 4, 2 * rows, 4 * group)

    def rows_at(zplace, by):
        block = lax.dynamic_slice(
            by_rows, (zplace, (x + by) % 4, 0, 0), (1, 1, 2 * rows, 4 * group)
        )
        return block[0, 0]

    def product_of(block):
        return jnp.dot(block, d_both, preferred_element_type=F32)

    steps = (2, 1, 3)
    away_got = [turned(product_of(rows_at(1 - zh, by)).astype(BF16), "x", by) for by in steps]
    near_parts = [product_of(rows_at(zh, by)).astype(BF16) for by in steps]

    def section(index):
        block = lax.dynamic_index_in_dim(mine, index % 4, 1, keepdims=False)
        return block.reshape(4 * own_rows, 2 * group)

    near_steps = (1, 3, 2)
    sends = [with_rows(section(sec + by), row) for by in near_steps]
    *near_parts, sends[0], sends[1], sends[2] = lax.optimization_barrier((*near_parts, *sends))
    got = [turned(s, "sec", by) for s, by in zip(sends, near_steps)]
    away_rows, got[0] = lax.optimization_barrier((rows_at(1 - zh, 0), got[0]))
    near_got = [turned(p, "x", by) for p, by in zip(near_parts, steps)]
    g_away = product_of(away_rows) + sum(g.astype(F32) for g in away_got)
    g_away = swapped(g_away.astype(BF16).reshape(2, rows, -1), "zh")

    total, row_total = section(sec), row
    for g in got:
        block, row_got = without_rows(g)
        total, row_total = total + block, row_total + row_got
    mine, row = total.reshape(4, own_rows, 2 * group), row_total
    sends = [with_rows(at(mine, (tp + by) % 4), row) for by in steps]
    got = [turned(s, "tp", by) for s, by in zip(sends, steps)]
    near_rows, *got = lax.optimization_barrier((rows_at(zh, 0), *got))
    g_near = product_of(near_rows) + sum(g.astype(F32) for g in near_got)
    g_near = g_near.astype(BF16).reshape(2, rows, -1)
    total, row_total = at(mine, tp), row
    for g in got:
        block, row_got = without_rows(g)
        total, row_total = total + block, row_total + row_got

    offset = (tp * 4 + sec) * own_rows
    own_inputs = lax.dynamic_slice_in_dim(inputs, offset, own_rows, 0).astype(F32)
    own_gain = lax.dynamic_slice_in_dim(norm_gain, offset, own_rows, 0)[:, None]
    grad_gain = jnp.sum(total * own_inputs * inv_rms, axis=1)
    send = with_rows(total[:, group:], row_total[group:])
    send, late_core = lax.optimization_barrier((send, core))
    got, row_got = without_rows(swapped(send, "zh"))
    grad_gain = grad_gain + swapped(grad_gain, "zh")
    keep = jnp.stack([at(g_near, core), at(g_away, late_core)])
    give = swapped(jnp.stack([at(g_near, 1 - core), at(g_away, 1 - late_core)]), "core")
    grad_gain = grad_gain + swapped(grad_gain, "core")
    grad_gain = grad_gain + sum(turned(grad_gain, "x", by) for by in steps)
    d_own, row_sum = total[:, :group] + got, row_total[:group] + row_got
    inv = inv_rms[:group]
    own_inputs = own_inputs[:, :group]
    grad_tokens = inv * own_gain * d_own - own_inputs * (inv**2 * row_sum / features)
    grad_gate, grad_up = joined(keep, give)
    return grad_tokens.T.astype(BF16), grad_gain, grad_gate, grad_up


def solution(mesh):
    split = Mesh(
        mesh.devices.reshape(2, 4, 2, mesh.shape["tp"], mesh.shape["section"]),
        (*DP, *COLS),
    )
    weights = P(DP, COLS)
    return jax.shard_map(
        shards,
        mesh=split,
        in_specs=(P(DP, "sec"), weights, P(), weights, weights),
        out_specs=(weights, P(COLS), weights, weights),
        check_vma=False,
    )
```

```python
import functools

import jax
import jax.numpy as jnp
from jax import lax
from jax.experimental import pallas as pl
from jax.experimental.pallas import tpu as pltpu
from jax.sharding import Mesh
from jax.sharding import PartitionSpec as P

DP = ("zh", "x", "core")
COLS = ("tp", "sec")
EPS = 1e-06
LANES = 128
EXTRA = 16
F32 = jnp.float32
BF16 = jnp.bfloat16
SDS = jax.ShapeDtypeStruct


def turned(array, axis, by):
    n = lax.axis_size(axis)
    return lax.ppermute(array, axis, [(i, (i + by) % n) for i in range(n)])


def swapped(array, axis):
    return turned(array, axis, 1)


def at(array, index):
    return lax.dynamic_index_in_dim(array, index, 0, keepdims=False)


def parts_of(width):
    main = width // LANES // 4 * LANES
    rest = width // 4 - main
    return main, rest


def pack_kernel(main, rest, aways, gate_ref, up_ref, back_ref, *outs):
    half = back_ref.shape[0] // 2
    zh, core = lax.axis_index("zh"), lax.axis_index("core")
    weights, backs = outs[:2], outs[2:]
    sources = (
        (weights, gate_ref, up_ref),
        (backs, back_ref.at[pl.ds(0, half)], back_ref.at[pl.ds(half, half)]),
    )
    for other in range(2):
        q = (zh ^ aways) * 2 + (core ^ other)
        wide = pl.ds(pl.multiple_of(q * main, LANES), main)
        for targets, first, second in sources:
            out = targets[other]
            out[:, pl.ds(0, main)] = first[:, wide]
            out[:, pl.ds(main, main)] = second[:, wide]
            thin = []
            for ref in (first, second):
                tail = ref[:, pl.ds(4 * main, 4 * rest)]
                pick = tail[:, :rest]
                for k in range(1, 4):
                    pick = jnp.where(q == k, tail[:, k * rest : (k + 1) * rest], pick)
                thin.append(pick)
            out[:, pl.ds(2 * main, 2 * rest)] = jnp.concatenate(thin, axis=1)


def packed(aways, w_gate, w_up, hidden_grad):
    rows, width = w_gate.shape
    main, rest = parts_of(width)
    block = pltpu.VMEM((rows, width // 2), BF16)
    back = pltpu.VMEM((hidden_grad.shape[0] // 2, width // 2), BF16)
    return pl.pallas_call(
        functools.partial(pack_kernel, main, rest, aways),
        out_shape=(block, block, back, back),
        in_specs=[pl.BlockSpec(memory_space=pltpu.VMEM)] * 3,
        out_specs=(pl.BlockSpec(memory_space=pltpu.VMEM),) * 4,
        name="pack",
    )(w_gate, w_up, hidden_grad)


def join_kernel(main, rest, keep_ref, give_ref, gate_ref, up_ref):
    zh, core = lax.axis_index("zh"), lax.axis_index("core")
    tails = [[None] * 4, [None] * 4]
    for aways in range(2):
        for other, ref in enumerate((keep_ref, give_ref)):
            q = (zh ^ aways) * 2 + (core ^ other)
            wide = pl.ds(pl.multiple_of(q * main, LANES), main)
            gate_ref[:, wide] = ref[aways, :, pl.ds(0, main)]
            up_ref[:, wide] = ref[aways, :, pl.ds(main, main)]
            tail = ref[aways, :, pl.ds(2 * main, 2 * rest)]
            for i in range(2):
                thin = tail[:, i * rest : (i + 1) * rest]
                for k in range(4):
                    old = tails[i][k]
                    tails[i][k] = thin if old is None else jnp.where(q == k, thin, old)
    gate_ref[:, pl.ds(4 * main, 4 * rest)] = jnp.concatenate(tails[0], axis=1)
    up_ref[:, pl.ds(4 * main, 4 * rest)] = jnp.concatenate(tails[1], axis=1)


def joined(keep, give):
    _, rows, half = keep.shape
    main, rest = parts_of(half * 2)
    out = SDS((rows, half * 2), BF16)
    return pl.pallas_call(
        functools.partial(join_kernel, main, rest),
        out_shape=(out, out),
        in_specs=[pl.BlockSpec(memory_space=pltpu.VMEM)] * 2,
        out_specs=(pl.BlockSpec(memory_space=pltpu.VMEM),) * 2,
        name="join",
    )(keep, give)


def split_pair(block):
    main, rest = parts_of(block.shape[1] * 2)
    first = jnp.concatenate([block[:, :main], block[:, 2 * main : 2 * main + rest]], axis=1)
    second = jnp.concatenate([block[:, main : 2 * main], block[:, 2 * main + rest :]], axis=1)
    return first, second


def join_pair(first, second):
    main, rest = parts_of(first.shape[1] * 4)
    return jnp.concatenate(
        [first[:, :main], second[:, :main], first[:, main:], second[:, main:]], axis=1
    )


def ordered(own, other, index):
    return jnp.where(index == 0, jnp.stack([own, other]), jnp.stack([other, own]))


def with_rows(block, row):
    high = row.astype(BF16)
    low = (row - high.astype(F32)).astype(BF16)
    tail = jnp.concatenate(
        [high[None], low[None], jnp.zeros((EXTRA - 2, row.shape[0]), BF16)], axis=0
    )
    return jnp.concatenate([block.astype(BF16).reshape(-1, row.shape[0]), tail], axis=0)


def without_rows(packed_rows):
    n = packed_rows.shape[0] - EXTRA
    wide = packed_rows.astype(F32)
    return wide[:n], wide[n] + wide[n + 1]


def derivatives(gate, up, back):
    hidden, pull = jax.vjp(lambda g, u: jax.nn.gelu(g, approximate=True) * u, gate, up)
    return pull(back)


def shards(tokens, hidden_grad, norm_gain, w_gate, w_up):
    rows, width = w_gate.shape
    group = tokens.shape[0]
    features = norm_gain.shape[0]
    own_rows = features // 16
    zh, x, core = (lax.axis_index(a) for a in DP)
    tp, sec = (lax.axis_index(a) for a in COLS)

    own_t = tokens.T
    far_t = swapped(own_t, "zh")

    away_own, away_other, back_away, back_cross = packed(1, w_gate, w_up, hidden_grad)
    hidden_grad, away_own = lax.optimization_barrier((hidden_grad, away_own))
    near_own, near_other, back_own, back_other = packed(0, w_gate, w_up, hidden_grad)
    away_own, away_other = swapped(away_own, "zh"), swapped(away_other, "zh")
    near_other, back_other = swapped(near_other, "core"), swapped(back_other, "core")

    full = jnp.zeros((2, 4, 2, rows, width // 2), BF16)

    def placed(full, pieces, zplace, cplace):
        for by, piece in zip((0, 1, 3, 2), pieces):
            piece = piece.reshape(1, 1, -1, rows, width // 2)
            full = lax.dynamic_update_slice(full, piece, (zplace, (x - by) % 4, cplace, 0, 0))
        return full

    pair = ordered(near_own, near_other, core)
    got = [turned(pair, "x", by) for by in (1, 3, 2)]
    backs = jnp.stack([back_away, back_cross])
    far_t, got[0], backs = lax.optimization_barrier((far_t, got[0], backs))
    full = placed(full, (pair, *got), zh, 0)
    backs = swapped(backs, "zh")

    both = jnp.concatenate([own_t, far_t], axis=1)
    both, away_own = lax.optimization_barrier((both, away_own))
    section_got = [turned(both, "sec", by) for by in (1, 3, 2)]
    own_got = [turned(away_own, "x", by) for by in (1, 3, 2)]

    inputs = jnp.zeros((4, *both.shape), BF16)
    for by, piece in zip((0, 1, 3, 2), (both, *section_got)):
        inputs = lax.dynamic_update_index_in_dim(inputs, piece, (sec - by) % 4, 0)
    inputs = inputs.reshape(features, 2 * group)
    wide = inputs.astype(F32)
    inv_rms = lax.rsqrt(jnp.mean(wide * wide, axis=0) + EPS)
    normed = (wide * inv_rms * norm_gain[:, None]).astype(BF16)
    normed, away_other, *own_got = lax.optimization_barrier((normed, away_other, *own_got))
    away_other = swapped(away_other, "core")
    normed = jnp.concatenate([normed, swapped(normed, "core")], axis=1)

    other_got = [turned(away_other, "x", by) for by in (1, 3, 2)]
    backs, *other_got = lax.optimization_barrier((backs, *other_got))
    full = placed(full, (away_own, *own_got), 1 - zh, core)
    full = placed(full, (away_other, *other_got), 1 - zh, 1 - core)
    full = full.reshape(features, -1)
    back = jnp.concatenate(
        [
            half
            for block in (back_own, backs[0], back_other, swapped(backs[1], "core"))
            for half in split_pair(block)
        ],
        axis=0,
    )

    product = lax.dot_general(
        normed, full, (((0,), (0,)), ((), ())), preferred_element_type=F32
    )
    gate, up = split_pair(product)
    d_gate, d_up = derivatives(gate, up, back.astype(F32))
    d_gate, d_up = d_gate.astype(BF16), d_up.astype(BF16)
    row_part = jnp.sum(d_gate.astype(F32) * gate + d_up.astype(F32) * up, axis=1)
    d_both = join_pair(d_gate, d_up)

    def d_normed(d):
        return lax.dot_general(full, d, (((1,), (1,)), ((), ())), preferred_element_type=F32)

    by_rows = normed.reshape(2, 4, 2 * rows, 4 * group)

    def rows_at(zplace, by):
        block = lax.dynamic_slice(
            by_rows, (zplace, (x + by) % 4, 0, 0), (1, 1, 2 * rows, 4 * group)
        )
        return block[0, 0]

    def product_of(block):
        return jnp.dot(block, d_both, preferred_element_type=F32)

    steps = (1, 3, 2)
    away_got = [turned(product_of(rows_at(1 - zh, by)).astype(BF16), "x", by) for by in steps]
    near_parts = [product_of(rows_at(zh, by)).astype(BF16) for by in steps]

    got = swapped(d_normed(d_both[2 * group :]).astype(BF16), "core")
    row = row_part[: 2 * group] + swapped(row_part[2 * group :], "core")
    mine = d_normed(d_both[: 2 * group]) + got.astype(F32)
    mine = mine.reshape(4, 4, own_rows, 2 * group)

    def section(index):
        block = lax.dynamic_index_in_dim(mine, index % 4, 1, keepdims=False)
        return block.reshape(4 * own_rows, 2 * group)

    sends = [with_rows(section(sec + by), row) for by in steps]
    away_got[0], away_got[1], *sends = lax.optimization_barrier(
        (away_got[0], away_got[1], *sends)
    )
    got = [turned(s, "sec", by) for s, by in zip(sends, steps)]
    away_got[2], *near_parts = lax.optimization_barrier((away_got[2], *near_parts))
    near_got = [turned(p, "x", by) for p, by in zip(near_parts, steps)]
    g_away = product_of(rows_at(1 - zh, 0)) + sum(g.astype(F32) for g in away_got)
    g_away, late_tp = lax.optimization_barrier((g_away.astype(BF16), tp))
    g_away = swapped(g_away.reshape(2, rows, -1), "zh")

    total, row_total = section(sec), row
    for g in got:
        block, row_got = without_rows(g)
        total, row_total = total + block, row_total + row_got
    mine, row = total.reshape(4, own_rows, 2 * group), row_total
    sends = [with_rows(at(mine, (late_tp + by) % 4), row) for by in steps]
    got = [turned(s, "tp", by) for s, by in zip(sends, steps)]
    near_rows, *got = lax.optimization_barrier((rows_at(zh, 0), *got))
    g_near = product_of(near_rows) + sum(g.astype(F32) for g in near_got)
    g_near = g_near.astype(BF16).reshape(2, rows, -1)
    total, row_total = at(mine, tp), row
    for g in got:
        block, row_got = without_rows(g)
        total, row_total = total + block, row_total + row_got

    offset = (tp * 4 + sec) * own_rows
    own_inputs = lax.dynamic_slice_in_dim(inputs, offset, own_rows, 0).astype(F32)
    own_gain = lax.dynamic_slice_in_dim(norm_gain, offset, own_rows, 0)[:, None]
    grad_gain = jnp.sum(total * own_inputs * inv_rms, axis=1)
    send = with_rows(total[:, group:], row_total[group:])
    got = swapped(send, "zh")
    grad_gain = grad_gain + swapped(grad_gain, "zh")
    got, grad_gain, late_core = lax.optimization_barrier((got, grad_gain, core))
    got, row_got = without_rows(got)
    keep = jnp.stack([at(g_near, core), at(g_away, late_core)])
    give = swapped(jnp.stack([at(g_near, 1 - core), at(g_away, 1 - late_core)]), "core")
    grad_gain = grad_gain + swapped(grad_gain, "core")
    grad_gain = grad_gain + sum(turned(grad_gain, "x", by) for by in steps)
    d_own, row_sum = total[:, :group] + got, row_total[:group] + row_got
    inv = inv_rms[:group]
    own_inputs = own_inputs[:, :group]
    grad_tokens = inv * own_gain * d_own - own_inputs * (inv**2 * row_sum / features)
    grad_gate, grad_up = joined(keep, give)
    return grad_tokens.T.astype(BF16), grad_gain, grad_gate, grad_up


def solution(mesh):
    split = Mesh(
        mesh.devices.reshape(2, 4, 2, mesh.shape["tp"], mesh.shape["section"]),
        (*DP, *COLS),
    )
    weights = P(DP, COLS)
    return jax.shard_map(
        shards,
        mesh=split,
        in_specs=(P(DP, "sec"), weights, P(), weights, weights),
        out_specs=(weights, P(COLS), weights, weights),
        check_vma=False,
    )
```

```python
import functools

import jax
import jax.numpy as jnp
from jax import lax
from jax.experimental import pallas as pl
from jax.experimental.pallas import tpu as pltpu
from jax.sharding import Mesh
from jax.sharding import PartitionSpec as P

DP = ("zh", "x", "core")
COLS = ("tp", "sec")
EPS = 1e-06
LANES = 128
EXTRA = 16
F32 = jnp.float32
BF16 = jnp.bfloat16
SDS = jax.ShapeDtypeStruct


def turned(array, axis, by):
    n = lax.axis_size(axis)
    return lax.ppermute(array, axis, [(i, (i + by) % n) for i in range(n)])


def swapped(array, axis):
    return turned(array, axis, 1)


def at(array, index):
    return lax.dynamic_index_in_dim(array, index, 0, keepdims=False)


def parts_of(width):
    main = width // LANES // 4 * LANES
    rest = width // 4 - main
    return main, rest


def pack_kernel(main, rest, rows, aways, gate_ref, up_ref, back_ref, *outs):
    half = back_ref.shape[0] // 2
    zh, core = lax.axis_index("zh"), lax.axis_index("core")
    sources = (
        (0, rows, gate_ref, up_ref),
        (rows, half, back_ref.at[pl.ds(0, half)], back_ref.at[pl.ds(half, half)]),
    )
    for other, out in enumerate(outs):
        q = (zh ^ aways) * 2 + (core ^ other)
        wide = pl.ds(pl.multiple_of(q * main, LANES), main)
        for start, count, first, second in sources:
            here = pl.ds(start, count)
            out[here, pl.ds(0, main)] = first[:, wide]
            out[here, pl.ds(main, main)] = second[:, wide]
            thin = []
            for ref in (first, second):
                tail = ref[:, pl.ds(4 * main, 4 * rest)]
                pick = tail[:, :rest]
                for k in range(1, 4):
                    pick = jnp.where(q == k, tail[:, k * rest : (k + 1) * rest], pick)
                thin.append(pick)
            out[here, pl.ds(2 * main, 2 * rest)] = jnp.concatenate(thin, axis=1)


def packed(aways, w_gate, w_up, hidden_grad):
    rows, width = w_gate.shape
    main, rest = parts_of(width)
    block = pltpu.VMEM((rows + hidden_grad.shape[0] // 2, width // 2), BF16)
    return pl.pallas_call(
        functools.partial(pack_kernel, main, rest, rows, aways),
        out_shape=(block,) * 2,
        in_specs=[pl.BlockSpec(memory_space=pltpu.VMEM)] * 3,
        out_specs=(pl.BlockSpec(memory_space=pltpu.VMEM),) * 2,
        name="pack",
    )(w_gate, w_up, hidden_grad)


def join_kernel(main, rest, keep_ref, give_ref, gate_ref, up_ref):
    zh, core = lax.axis_index("zh"), lax.axis_index("core")
    tails = [[None] * 4, [None] * 4]
    for aways in range(2):
        for other, ref in enumerate((keep_ref, give_ref)):
            q = (zh ^ aways) * 2 + (core ^ other)
            wide = pl.ds(pl.multiple_of(q * main, LANES), main)
            gate_ref[:, wide] = ref[aways, :, pl.ds(0, main)]
            up_ref[:, wide] = ref[aways, :, pl.ds(main, main)]
            tail = ref[aways, :, pl.ds(2 * main, 2 * rest)]
            for i in range(2):
                thin = tail[:, i * rest : (i + 1) * rest]
                for k in range(4):
                    old = tails[i][k]
                    tails[i][k] = thin if old is None else jnp.where(q == k, thin, old)
    gate_ref[:, pl.ds(4 * main, 4 * rest)] = jnp.concatenate(tails[0], axis=1)
    up_ref[:, pl.ds(4 * main, 4 * rest)] = jnp.concatenate(tails[1], axis=1)


def joined(keep, give):
    _, rows, half = keep.shape
    main, rest = parts_of(half * 2)
    out = SDS((rows, half * 2), BF16)
    return pl.pallas_call(
        functools.partial(join_kernel, main, rest),
        out_shape=(out, out),
        in_specs=[pl.BlockSpec(memory_space=pltpu.VMEM)] * 2,
        out_specs=(pl.BlockSpec(memory_space=pltpu.VMEM),) * 2,
        name="join",
    )(keep, give)


def split_pair(block):
    main, rest = parts_of(block.shape[1] * 2)
    first = jnp.concatenate([block[:, :main], block[:, 2 * main : 2 * main + rest]], axis=1)
    second = jnp.concatenate([block[:, main : 2 * main], block[:, 2 * main + rest :]], axis=1)
    return first, second


def join_pair(first, second):
    main, rest = parts_of(first.shape[1] * 4)
    return jnp.concatenate(
        [first[:, :main], second[:, :main], first[:, main:], second[:, main:]], axis=1
    )


def ordered(own, other, index):
    return jnp.where(index == 0, jnp.stack([own, other]), jnp.stack([other, own]))


def halves(row):
    high = row.astype(BF16)
    return high, (row - high.astype(F32)).astype(BF16)


def with_rows(block, *rows):
    width = block.shape[1]
    tail = [half.reshape(1, width) for row in rows for half in halves(row)]
    tail.append(jnp.zeros((EXTRA - len(tail), width), BF16))
    return jnp.concatenate([block.astype(BF16), *tail], axis=0)


def row_of(packed_rows, k=0):
    at_row = packed_rows.shape[0] - EXTRA + 2 * k
    return packed_rows[at_row].astype(F32) + packed_rows[at_row + 1].astype(F32)


def block_of(packed_rows):
    return packed_rows[: packed_rows.shape[0] - EXTRA].astype(F32)


def derivatives(gate, up, back):
    hidden, pull = jax.vjp(lambda g, u: jax.nn.gelu(g, approximate=True) * u, gate, up)
    return pull(back)


def shards(tokens, hidden_grad, norm_gain, w_gate, w_up):
    rows, width = w_gate.shape
    group = tokens.shape[0]
    features = norm_gain.shape[0]
    own_rows = features // 16
    zh, x, core = (lax.axis_index(a) for a in DP)
    tp, sec = (lax.axis_index(a) for a in COLS)

    own_t = tokens.T
    far_t = swapped(own_t, "zh")

    away_own, away_other = packed(1, w_gate, w_up, hidden_grad)
    hidden_grad, away_own = lax.optimization_barrier((hidden_grad, away_own))
    near_own, near_other = packed(0, w_gate, w_up, hidden_grad)
    away_own, away_other = swapped(away_own, "zh"), swapped(away_other, "zh")
    near_other = swapped(near_other, "core")

    near = ordered(near_own[:rows], near_other[:rows], core)
    near, far_t = lax.optimization_barrier((near, far_t))
    near_got = [turned(near, "x", by) for by in (1, 3, 2)]

    both = jnp.concatenate([own_t, far_t], axis=1)
    section_got = [turned(both, "sec", by) for by in (1, 3, 2)]

    away_other = swapped(away_other, "core")
    near_got[0], near_got[1], late_core = lax.optimization_barrier(
        (near_got[0], near_got[1], core)
    )
    away = ordered(away_own[:rows], away_other[:rows], late_core)
    away, late_sec = lax.optimization_barrier((away, sec))
    away_got = [turned(away, "x", by) for by in (1, 3, 2)]

    inputs = jnp.zeros((4, *both.shape), BF16)
    for by, piece in zip((0, 1, 3, 2), (both, *section_got)):
        inputs = lax.dynamic_update_index_in_dim(inputs, piece, (late_sec - by) % 4, 0)
    inputs = inputs.reshape(features, 2 * group)
    wide = inputs.astype(F32)
    inv_rms = lax.rsqrt(jnp.mean(wide * wide, axis=0) + EPS)
    normed = (wide * inv_rms * norm_gain[:, None]).astype(BF16)
    normed, *near_got = lax.optimization_barrier((normed, *near_got))
    normed = jnp.concatenate([normed, swapped(normed, "core")], axis=1)

    full = jnp.zeros((2, 4, 2, rows, width // 2), BF16)
    for pieces, place in (((near, *near_got), zh), ((away, *away_got), 1 - zh)):
        for by, piece in zip((0, 1, 3, 2), pieces):
            full = lax.dynamic_update_slice(
                full, piece[None, None], (place, (x - by) % 4, 0, 0, 0)
            )
    full = full.reshape(features, -1)
    back = jnp.concatenate(
        [
            half
            for block in (near_own, away_own, near_other, away_other)
            for half in split_pair(block[rows:])
        ],
        axis=0,
    )

    product = lax.dot_general(
        normed, full, (((0,), (0,)), ((), ())), preferred_element_type=F32
    )
    gate, up = split_pair(product)
    d_gate, d_up = derivatives(gate, up, back.astype(F32))
    d_gate, d_up = d_gate.astype(BF16), d_up.astype(BF16)
    row_part = jnp.sum(d_gate.astype(F32) * gate + d_up.astype(F32) * up, axis=1)
    d_both = join_pair(d_gate, d_up)

    def d_normed(d):
        return lax.dot_general(full, d, (((1,), (1,)), ((), ())), preferred_element_type=F32)

    by_rows = normed.reshape(2, 4, 2 * rows, 4 * group)

    def rows_at(zplace, by):
        block = lax.dynamic_slice(
            by_rows, (zplace, (x + by) % 4, 0, 0), (1, 1, 2 * rows, 4 * group)
        )
        return block[0, 0]

    def product_of(block):
        return jnp.dot(block, d_both, preferred_element_type=F32)

    steps = (1, 3, 2)
    away_got = [turned(product_of(rows_at(1 - zh, by)).astype(BF16), "x", by) for by in steps]
    near_parts = [product_of(rows_at(zh, by)).astype(BF16) for by in steps]

    got = swapped(d_normed(d_both[2 * group :]).astype(BF16), "core")
    row = row_part[: 2 * group] + swapped(row_part[2 * group :], "core")
    mine = d_normed(d_both[: 2 * group]) + got.astype(F32)
    mine = mine.reshape(4, 4, own_rows, 2 * group)

    def section(index):
        block = lax.dynamic_index_in_dim(mine, index % 4, 1, keepdims=False)
        return block.reshape(4 * own_rows, 2 * group)

    sends = [with_rows(section(sec + by), row) for by in steps]
    away_got[0], *sends = lax.optimization_barrier((away_got[0], *sends))
    got = [turned(s, "sec", by) for s, by in zip(sends, steps)]
    *away_got, near_parts[0], near_parts[1], near_parts[2] = lax.optimization_barrier(
        (*away_got, *near_parts)
    )
    near_got = [turned(p, "x", by) for p, by in zip(near_parts, steps)]
    g_away = product_of(rows_at(1 - zh, 0)) + sum(g.astype(F32) for g in away_got)
    g_away = g_away.astype(BF16).reshape(2, rows, -1)
    near_got[0], near_got[1], g_away, late_tp = lax.optimization_barrier(
        (near_got[0], near_got[1], g_away, tp)
    )
    away_keep = swapped(at(g_away, core), "zh")
    away_give = swapped(at(g_away, 1 - core), "zh")

    total = section(sec) + sum(block_of(g) for g in got)
    row = row + sum(row_of(g) for g in got)
    mine = total.reshape(4, own_rows, 2 * group)
    sends = [with_rows(at(mine, (late_tp + by) % 4), row) for by in steps]
    got = [turned(s, "tp", by) for s, by in zip(sends, steps)]
    near_rows, *got = lax.optimization_barrier((rows_at(zh, 0), *got))
    g_near = product_of(near_rows) + sum(g.astype(F32) for g in near_got)
    g_near = g_near.astype(BF16).reshape(2, rows, -1)
    total = at(mine, tp) + sum(block_of(g) for g in got)
    row = row + sum(row_of(g) for g in got)

    offset = (tp * 4 + sec) * own_rows
    own_inputs = lax.dynamic_slice_in_dim(inputs, offset, own_rows, 0).astype(F32)
    own_gain = lax.dynamic_slice_in_dim(norm_gain, offset, own_rows, 0)[:, None]
    gain_part = jnp.sum(total * own_inputs * inv_rms, axis=1)
    gain_rows = jnp.pad(gain_part, (0, 2 * group - own_rows)).reshape(2, group)
    send = with_rows(total[:, group:], row[group:], gain_rows[0], gain_rows[1])
    send, away_give = lax.optimization_barrier((send, away_give))
    got = swapped(send, "zh")
    give = swapped(jnp.stack([at(g_near, 1 - core), away_give]), "core")
    grad_gain = gain_part + jnp.concatenate([row_of(got, 1), row_of(got, 2)])[:own_rows]
    grad_gain = grad_gain + swapped(grad_gain, "core")
    grad_gain = grad_gain + sum(turned(grad_gain, "x", by) for by in steps)
    d_own, row_sum = total[:, :group] + block_of(got), row[:group] + row_of(got)
    inv = inv_rms[:group]
    own_inputs = own_inputs[:, :group]
    grad_tokens = inv * own_gain * d_own - own_inputs * (inv**2 * row_sum / features)
    grad_gate, grad_up = joined(jnp.stack([at(g_near, core), away_keep]), give)
    return grad_tokens.T.astype(BF16), grad_gain, grad_gate, grad_up


def solution(mesh):
    split = Mesh(
        mesh.devices.reshape(2, 4, 2, mesh.shape["tp"], mesh.shape["section"]),
        (*DP, *COLS),
    )
    weights = P(DP, COLS)
    return jax.shard_map(
        shards,
        mesh=split,
        in_specs=(P(DP, "sec"), weights, P(), weights, weights),
        out_specs=(weights, P(COLS), weights, weights),
        check_vma=False,
    )
```

```python
import functools

import jax
import jax.numpy as jnp
from jax import lax
from jax.experimental import pallas as pl
from jax.experimental.pallas import tpu as pltpu
from jax.sharding import Mesh
from jax.sharding import PartitionSpec as P

DP = ("zh", "x", "core")
COLS = ("tp", "sec")
EPS = 1e-06
LANES = 128
EXTRA = 16
F32 = jnp.float32
BF16 = jnp.bfloat16
SDS = jax.ShapeDtypeStruct


def turned(array, axis, by):
    n = lax.axis_size(axis)
    return lax.ppermute(array, axis, [(i, (i + by) % n) for i in range(n)])


def swapped(array, axis):
    return turned(array, axis, 1)


def unsigned(index):
    return index.astype(jnp.uint32)


def as_block(array, *lead):
    n = len(lead)
    zeros = [jnp.uint32(0)] * (array.ndim - n)
    part = lax.dynamic_slice(array, (*lead, *zeros), (*([1] * n), *array.shape[n:]))
    return part.reshape(array.shape[n:])


def put(array, part, *lead):
    zeros = [jnp.uint32(0)] * (array.ndim - len(lead))
    part = part.reshape(*([1] * len(lead)), *array.shape[len(lead) :])
    return lax.dynamic_update_slice(array, part, (*lead, *zeros))


def parts_of(width):
    main = width // LANES // 4 * LANES
    rest = width // 4 - main
    return main, rest


def pack_kernel(main, rest, aways, gate_ref, up_ref, back_ref, *outs):
    half = back_ref.shape[0] // 2
    zh, core = lax.axis_index("zh"), lax.axis_index("core")
    weights, backs = outs[:2], outs[2:]
    if aways:
        backs = [outs[2].at[0], outs[2].at[1]]
    sources = (
        (weights, gate_ref, up_ref),
        (backs, back_ref.at[pl.ds(0, half)], back_ref.at[pl.ds(half, half)]),
    )
    for other in range(2):
        q = (zh ^ aways) * 2 + (core ^ other)
        wide = pl.ds(pl.multiple_of(q * main, LANES), main)
        for targets, first, second in sources:
            out = targets[other]
            out[:, pl.ds(0, main)] = first[:, wide]
            out[:, pl.ds(main, main)] = second[:, wide]
            thin = []
            for ref in (first, second):
                tail = ref[:, pl.ds(4 * main, 4 * rest)]
                pick = tail[:, :rest]
                for k in range(1, 4):
                    pick = jnp.where(q == k, tail[:, k * rest : (k + 1) * rest], pick)
                thin.append(pick)
            out[:, pl.ds(2 * main, 2 * rest)] = jnp.concatenate(thin, axis=1)


def packed(aways, w_gate, w_up, hidden_grad):
    rows, width = w_gate.shape
    main, rest = parts_of(width)
    block = pltpu.VMEM((rows, width // 2), BF16)
    shape = (hidden_grad.shape[0] // 2, width // 2)
    backs = [pltpu.VMEM((2, *shape), BF16)] if aways else [pltpu.VMEM(shape, BF16)] * 2
    return pl.pallas_call(
        functools.partial(pack_kernel, main, rest, aways),
        out_shape=(block, block, *backs),
        in_specs=[pl.BlockSpec(memory_space=pltpu.VMEM)] * 3,
        out_specs=(pl.BlockSpec(memory_space=pltpu.VMEM),) * (2 + len(backs)),
        name="pack",
    )(w_gate, w_up, hidden_grad)


def join_kernel(main, rest, near_ref, keep_ref, give_ref, gate_ref, up_ref):
    zh, core = lax.axis_index("zh"), lax.axis_index("core")
    tails = [[None] * 4, [None] * 4]
    for aways in range(2):
        for other in range(2):
            ref = give_ref.at[aways] if other else keep_ref if aways else near_ref.at[core]
            q = (zh ^ aways) * 2 + (core ^ other)
            wide = pl.ds(pl.multiple_of(q * main, LANES), main)
            gate_ref[:, wide] = ref[:, pl.ds(0, main)]
            up_ref[:, wide] = ref[:, pl.ds(main, main)]
            tail = ref[:, pl.ds(2 * main, 2 * rest)]
            for i in range(2):
                thin = tail[:, i * rest : (i + 1) * rest]
                for k in range(4):
                    old = tails[i][k]
                    tails[i][k] = thin if old is None else jnp.where(q == k, thin, old)
    gate_ref[:, pl.ds(4 * main, 4 * rest)] = jnp.concatenate(tails[0], axis=1)
    up_ref[:, pl.ds(4 * main, 4 * rest)] = jnp.concatenate(tails[1], axis=1)


def joined(near, keep, give):
    rows, half = keep.shape
    main, rest = parts_of(half * 2)
    out = SDS((rows, half * 2), BF16)
    return pl.pallas_call(
        functools.partial(join_kernel, main, rest),
        out_shape=(out, out),
        in_specs=[pl.BlockSpec(memory_space=pltpu.VMEM)] * 3,
        out_specs=(pl.BlockSpec(memory_space=pltpu.VMEM),) * 2,
        name="join",
    )(near, keep, give)


def split_pair(block):
    main, rest = parts_of(block.shape[1] * 2)
    first = jnp.concatenate([block[:, :main], block[:, 2 * main : 2 * main + rest]], axis=1)
    second = jnp.concatenate([block[:, main : 2 * main], block[:, 2 * main + rest :]], axis=1)
    return first, second


def join_pair(first, second):
    main, rest = parts_of(first.shape[1] * 4)
    return jnp.concatenate(
        [first[:, :main], second[:, :main], first[:, main:], second[:, main:]], axis=1
    )


def ordered(own, other, first):
    return jnp.where(first, jnp.stack([own, other]), jnp.stack([other, own]))


def halves(row):
    high = row.astype(BF16)
    return high, (row - high.astype(F32)).astype(BF16)


def with_rows(block, *rows):
    shape = (EXTRA, block.shape[1])
    which = lax.broadcasted_iota(jnp.int32, shape, 0)
    tail = jnp.zeros(shape, BF16)
    for k, half in enumerate([half for row in rows for half in halves(row)]):
        tail = jnp.where(which == k, half[None, :], tail)
    return jnp.concatenate([block.astype(BF16), tail], axis=0)


def row_of(packed_rows, k=0):
    at_row = packed_rows.shape[0] - EXTRA + 2 * k
    return packed_rows[at_row].astype(F32) + packed_rows[at_row + 1].astype(F32)


def block_of(packed_rows):
    return packed_rows[: packed_rows.shape[0] - EXTRA].astype(F32)


def derivatives(gate, up, back):
    hidden, pull = jax.vjp(lambda g, u: jax.nn.gelu(g, approximate=True) * u, gate, up)
    return pull(back)


def shards(tokens, hidden_grad, norm_gain, w_gate, w_up):
    rows, width = w_gate.shape
    group = tokens.shape[0]
    features = norm_gain.shape[0]
    own_rows = features // 16
    barrier = lax.optimization_barrier

    zh, x, core, tp, sec = (unsigned(lax.axis_index(a)) for a in (*DP, *COLS))
    steps = (1, 3, 2)
    far_zh, other_core = 1 - zh, 1 - core
    first_core = core == 0
    x_to = {by: (x + by) & 3 for by in range(4)}
    sec_to = {by: (sec + by) & 3 for by in range(4)}
    tp_to = {by: (tp + by) & 3 for by in range(4)}
    offset = (tp * 4 + sec) * own_rows

    own_t = tokens.T
    far_t = swapped(own_t, "zh")

    away_own, away_other, backs = packed(1, w_gate, w_up, hidden_grad)
    hidden_grad, away_own = barrier((hidden_grad, away_own))
    near_own, near_other, back_own, back_other = packed(0, w_gate, w_up, hidden_grad)
    away_own, away_other = swapped(away_own, "zh"), swapped(away_other, "zh")
    near_other, back_other = swapped(near_other, "core"), swapped(back_other, "core")

    near = ordered(near_own, near_other, first_core)
    near, far_t = barrier((near, far_t))
    near_got = [turned(near, "x", by) for by in steps]

    both = jnp.concatenate([own_t, far_t], axis=1)
    section_got = [turned(both, "sec", by) for by in steps]

    away_other = swapped(away_other, "core")
    *near_got, late_first = barrier((*near_got, first_core))
    backs, near_got[0] = barrier((backs, near_got[0]))
    backs = swapped(backs, "zh")
    away = ordered(away_own, away_other, late_first)
    late = {}
    away, late[0], late[1], late[2], late[3] = barrier((away, *(sec_to[by] for by in range(4))))
    away_got = [turned(away, "x", by) for by in steps]

    inputs = jnp.zeros((4, *both.shape), BF16)
    for by, piece in zip((0, 3, 1, 2), (both, *section_got)):
        inputs = put(inputs, piece, late[by])
    inputs = inputs.reshape(features, 2 * group)
    wide = inputs.astype(F32)
    inv_rms = lax.rsqrt(jnp.mean(wide * wide, axis=0) + EPS)
    normed = (wide * inv_rms * norm_gain[:, None]).astype(BF16)
    normed = jnp.concatenate([normed, swapped(normed, "core")], axis=1)

    full = jnp.zeros((2, 4, 2, rows, width // 2), BF16)
    for pieces, place in (((near, *near_got), zh), ((away, *away_got), far_zh)):
        for by, piece in zip((0, 3, 1, 2), pieces):
            full = put(full, piece, place, x_to[by])
    full = full.reshape(features, -1)
    back = jnp.concatenate(
        [
            half
            for block in (back_own, backs[0], back_other, swapped(backs[1], "core"))
            for half in split_pair(block)
        ],
        axis=0,
    )

    product = lax.dot_general(
        normed, full, (((0,), (0,)), ((), ())), preferred_element_type=F32
    )
    gate, up = split_pair(product)
    d_gate, d_up = derivatives(gate, up, back.astype(F32))
    d_gate, d_up = d_gate.astype(BF16), d_up.astype(BF16)
    row_part = jnp.sum(d_gate.astype(F32) * gate + d_up.astype(F32) * up, axis=1)
    d_both = join_pair(d_gate, d_up)

    def d_normed(d):
        return lax.dot_general(full, d, (((1,), (1,)), ((), ())), preferred_element_type=F32)

    by_rows = normed.reshape(2, 4, 2 * rows, 4 * group)

    def part(zplace, xplace):
        return jnp.dot(as_block(by_rows, zplace, xplace), d_both, preferred_element_type=F32)

    away_parts = [part(far_zh, x_to[by]).astype(BF16) for by in steps]
    near_parts = [part(zh, x_to[by]).astype(BF16) for by in steps]
    away_got = [turned(away_parts[0], "x", 1)]

    got = swapped(d_normed(d_both[2 * group :]).astype(BF16), "core")
    row = row_part[: 2 * group] + swapped(row_part[2 * group :], "core")
    got, away_parts[1], away_parts[2] = barrier((got, away_parts[1], away_parts[2]))
    away_got += [turned(away_parts[k], "x", steps[k]) for k in (1, 2)]
    mine = d_normed(d_both[: 2 * group]) + got.astype(F32)
    mine = mine.reshape(4, 4, own_rows, 2 * group)

    def section(index):
        zero = jnp.uint32(0)
        block = lax.dynamic_slice(
            mine, (zero, index, zero, zero), (4, 1, own_rows, 2 * group)
        )
        return block.reshape(4 * own_rows, 2 * group)

    sends = [with_rows(section(sec_to[by]), row) for by in steps]
    away_got[0], *sends = barrier((away_got[0], *sends))
    got = [turned(s, "sec", by) for s, by in zip(sends, steps)]
    away_got[1], away_got[2], *near_parts = barrier((away_got[1], away_got[2], *near_parts))
    near_got = [turned(p, "x", by) for p, by in zip(near_parts, steps)]
    g_away = part(far_zh, x) + sum(g.astype(F32) for g in away_got)
    g_away = g_away.astype(BF16).reshape(2, rows, -1)
    late = {}
    g_away, late[1], late[3], late[2] = barrier((g_away, *(tp_to[by] for by in steps)))
    away_keep = swapped(as_block(g_away, core), "zh")
    away_give = swapped(as_block(g_away, other_core), "zh")

    total = section(sec) + sum(block_of(g) for g in got)
    row = row + sum(row_of(g) for g in got)
    mine = total.reshape(4, own_rows, 2 * group)
    sends = [with_rows(as_block(mine, late[by]), row) for by in steps]
    got = [turned(s, "tp", by) for s, by in zip(sends, steps)]
    total = as_block(mine, tp) + sum(block_of(g) for g in got)
    row = row + sum(row_of(g) for g in got)

    own_inputs = lax.dynamic_slice(inputs, (offset, jnp.uint32(0)), (own_rows, 2 * group))
    own_inputs = own_inputs.astype(F32)
    own_gain = lax.dynamic_slice(norm_gain, (offset,), (own_rows,))[:, None]
    gain_part = jnp.sum(total * own_inputs * inv_rms, axis=1)
    gain_rows = jnp.pad(gain_part, (0, 2 * group - own_rows)).reshape(2, group)
    send = with_rows(total[:, group:], row[group:], gain_rows[0], gain_rows[1])
    send, near_got[0], near_got[1], late_zh = barrier((send, near_got[0], near_got[1], zh))
    got = swapped(send, "zh")
    g_near = part(late_zh, x) + sum(g.astype(F32) for g in near_got)
    g_near = g_near.astype(BF16).reshape(2, rows, -1)
    give = swapped(jnp.stack([as_block(g_near, other_core), away_give]), "core")
    grad_gain = gain_part + jnp.concatenate([row_of(got, 1), row_of(got, 2)])[:own_rows]
    grad_gain = grad_gain + swapped(grad_gain, "core")
    grad_gain = grad_gain + sum(turned(grad_gain, "x", by) for by in steps)
    d_own, row_sum = total[:, :group] + block_of(got), row[:group] + row_of(got)
    inv = inv_rms[:group]
    own_inputs = own_inputs[:, :group]
    grad_tokens = inv * own_gain * d_own - own_inputs * (inv**2 * row_sum / features)
    grad_gate, grad_up = joined(g_near, away_keep, give)
    return grad_tokens.T.astype(BF16), grad_gain, grad_gate, grad_up


def solution(mesh):
    split = Mesh(
        mesh.devices.reshape(2, 4, 2, mesh.shape["tp"], mesh.shape["section"]),
        (*DP, *COLS),
    )
    weights = P(DP, COLS)
    return jax.shard_map(
        shards,
        mesh=split,
        in_specs=(P(DP, "sec"), weights, P(), weights, weights),
        out_specs=(weights, P(COLS), weights, weights),
        check_vma=False,
    )
```

```python
import functools

import jax
import jax.numpy as jnp
from jax import lax
from jax.experimental import pallas as pl
from jax.experimental.pallas import tpu as pltpu
from jax.sharding import Mesh
from jax.sharding import PartitionSpec as P

DP = ("zh", "x", "core")
COLS = ("tp", "sec")
EPS = 1e-06
LANES = 128
EXTRA = 16
F32 = jnp.float32
BF16 = jnp.bfloat16
SDS = jax.ShapeDtypeStruct


def turned(array, axis, by):
    n = lax.axis_size(axis)
    return lax.ppermute(array, axis, [(i, (i + by) % n) for i in range(n)])


def swapped(array, axis):
    return turned(array, axis, 1)


def unsigned(index):
    return index.astype(jnp.uint32)


def as_block(array, *lead):
    n = len(lead)
    zeros = [jnp.uint32(0)] * (array.ndim - n)
    part = lax.dynamic_slice(array, (*lead, *zeros), (*([1] * n), *array.shape[n:]))
    return part.reshape(array.shape[n:])


def put(array, part, *lead):
    zeros = [jnp.uint32(0)] * (array.ndim - len(lead))
    part = part.reshape(*([1] * len(lead)), *array.shape[len(lead) :])
    return lax.dynamic_update_slice(array, part, (*lead, *zeros))


def parts_of(width):
    main = width // LANES // 4 * LANES
    rest = width // 4 - main
    return main, rest


def pack_kernel(main, rest, aways, gate_ref, up_ref, back_ref, *outs):
    half = back_ref.shape[0] // 2
    zh, core = lax.axis_index("zh"), lax.axis_index("core")
    rows = gate_ref.shape[0]
    if aways:
        weights, backs = outs[:2], [outs[2].at[0], outs[2].at[1]]
    else:
        weights = [out.at[pl.ds(0, rows)] for out in outs]
        backs = [out.at[pl.ds(rows, half)] for out in outs]
    sources = (
        (weights, gate_ref, up_ref),
        (backs, back_ref.at[pl.ds(0, half)], back_ref.at[pl.ds(half, half)]),
    )
    for other in range(2):
        q = (zh ^ aways) * 2 + (core ^ other)
        wide = pl.ds(pl.multiple_of(q * main, LANES), main)
        for targets, first, second in sources:
            out = targets[other]
            out[:, pl.ds(0, main)] = first[:, wide]
            out[:, pl.ds(main, main)] = second[:, wide]
            thin = []
            for ref in (first, second):
                tail = ref[:, pl.ds(4 * main, 4 * rest)]
                pick = tail[:, :rest]
                for k in range(1, 4):
                    pick = jnp.where(q == k, tail[:, k * rest : (k + 1) * rest], pick)
                thin.append(pick)
            out[:, pl.ds(2 * main, 2 * rest)] = jnp.concatenate(thin, axis=1)


def packed(aways, w_gate, w_up, hidden_grad):
    rows, width = w_gate.shape
    main, rest = parts_of(width)
    half = hidden_grad.shape[0] // 2
    if aways:
        outs = [(rows, width // 2), (rows, width // 2), (2, half, width // 2)]
    else:
        outs = [(rows + half, width // 2)] * 2
    return pl.pallas_call(
        functools.partial(pack_kernel, main, rest, aways),
        out_shape=[pltpu.VMEM(shape, BF16) for shape in outs],
        in_specs=[pl.BlockSpec(memory_space=pltpu.VMEM)] * 3,
        out_specs=[pl.BlockSpec(memory_space=pltpu.VMEM)] * len(outs),
        name="pack",
    )(w_gate, w_up, hidden_grad)


def join_kernel(main, rest, near_ref, keep_ref, give_ref, gate_ref, up_ref):
    zh, core = lax.axis_index("zh"), lax.axis_index("core")
    tails = [[None] * 4, [None] * 4]
    for aways in range(2):
        for other in range(2):
            ref = give_ref.at[aways] if other else keep_ref if aways else near_ref.at[core]
            q = (zh ^ aways) * 2 + (core ^ other)
            wide = pl.ds(pl.multiple_of(q * main, LANES), main)
            gate_ref[:, wide] = ref[:, pl.ds(0, main)]
            up_ref[:, wide] = ref[:, pl.ds(main, main)]
            tail = ref[:, pl.ds(2 * main, 2 * rest)]
            for i in range(2):
                thin = tail[:, i * rest : (i + 1) * rest]
                for k in range(4):
                    old = tails[i][k]
                    tails[i][k] = thin if old is None else jnp.where(q == k, thin, old)
    gate_ref[:, pl.ds(4 * main, 4 * rest)] = jnp.concatenate(tails[0], axis=1)
    up_ref[:, pl.ds(4 * main, 4 * rest)] = jnp.concatenate(tails[1], axis=1)


def joined(near, keep, give):
    rows, half = keep.shape
    main, rest = parts_of(half * 2)
    out = SDS((rows, half * 2), BF16)
    return pl.pallas_call(
        functools.partial(join_kernel, main, rest),
        out_shape=(out, out),
        in_specs=[pl.BlockSpec(memory_space=pltpu.VMEM)] * 3,
        out_specs=(pl.BlockSpec(memory_space=pltpu.VMEM),) * 2,
        name="join",
    )(near, keep, give)


def split_pair(block):
    main, rest = parts_of(block.shape[1] * 2)
    first = jnp.concatenate([block[:, :main], block[:, 2 * main : 2 * main + rest]], axis=1)
    second = jnp.concatenate([block[:, main : 2 * main], block[:, 2 * main + rest :]], axis=1)
    return first, second


def join_pair(first, second):
    main, rest = parts_of(first.shape[1] * 4)
    return jnp.concatenate(
        [first[:, :main], second[:, :main], first[:, main:], second[:, main:]], axis=1
    )


def ordered(own, other, first):
    return jnp.where(first, jnp.stack([own, other]), jnp.stack([other, own]))


def halves(row):
    high = row.astype(BF16)
    return high, (row - high.astype(F32)).astype(BF16)


def with_rows(block, *rows):
    shape = (EXTRA, block.shape[1])
    which = lax.broadcasted_iota(jnp.int32, shape, 0)
    tail = jnp.zeros(shape, BF16)
    for k, half in enumerate([half for row in rows for half in halves(row)]):
        tail = jnp.where(which == k, half[None, :], tail)
    return jnp.concatenate([block.astype(BF16), tail], axis=0)


def row_of(packed_rows, k=0):
    at_row = packed_rows.shape[0] - EXTRA + 2 * k
    return packed_rows[at_row].astype(F32) + packed_rows[at_row + 1].astype(F32)


def block_of(packed_rows):
    return packed_rows[: packed_rows.shape[0] - EXTRA].astype(F32)


def derivatives(gate, up, back):
    hidden, pull = jax.vjp(lambda g, u: jax.nn.gelu(g, approximate=True) * u, gate, up)
    return pull(back)


def shards(tokens, hidden_grad, norm_gain, w_gate, w_up):
    rows, width = w_gate.shape
    group = tokens.shape[0]
    features = norm_gain.shape[0]
    own_rows = features // 16
    barrier = lax.optimization_barrier

    zh, x, core, tp, sec = (unsigned(lax.axis_index(a)) for a in (*DP, *COLS))
    steps = (1, 3, 2)
    far_zh, other_core = 1 - zh, 1 - core
    first_core = core == 0
    x_to = {by: (x + by) & 3 for by in range(4)}
    sec_to = {by: (sec + by) & 3 for by in range(4)}
    tp_to = {by: (tp + by) & 3 for by in range(4)}
    offset = (tp * 4 + sec) * own_rows

    own_t = tokens.T
    far_t = swapped(own_t, "zh")

    near_own, near_other = packed(0, w_gate, w_up, hidden_grad)
    hidden_grad, near_own = barrier((hidden_grad, near_own))
    away_own, away_other, backs = packed(1, w_gate, w_up, hidden_grad)
    near_other = swapped(near_other, "core")
    away_other, far_t = barrier((away_other, far_t))
    away_own, away_other = swapped(away_own, "zh"), swapped(away_other, "zh")

    near = ordered(near_own[:rows], near_other[:rows], first_core)
    near, own_t = barrier((near, own_t))
    near_got = [turned(near, "x", by) for by in steps]

    both = jnp.concatenate([own_t, far_t], axis=1)
    section_got = [turned(both, "sec", by) for by in steps]

    near_got[0], near_got[1], backs, late_first = barrier(
        (near_got[0], near_got[1], backs, first_core)
    )
    away_other = swapped(away_other, "core")
    backs = swapped(backs, "zh")
    away = ordered(away_own, away_other, late_first)
    late = {}
    away, late[0], late[1], late[2], late[3] = barrier((away, *(sec_to[by] for by in range(4))))
    away_got = [turned(away, "x", by) for by in steps]

    inputs = jnp.zeros((4, *both.shape), BF16)
    for by, piece in zip((0, 3, 1, 2), (both, *section_got)):
        inputs = put(inputs, piece, late[by])
    inputs = inputs.reshape(features, 2 * group)
    wide = inputs.astype(F32)
    inv_rms = lax.rsqrt(jnp.mean(wide * wide, axis=0) + EPS)
    normed = (wide * inv_rms * norm_gain[:, None]).astype(BF16)
    normed, away_got[0] = barrier((normed, away_got[0]))
    normed = jnp.concatenate([normed, swapped(normed, "core")], axis=1)

    backs, *away_got = barrier((backs, *away_got))
    full = jnp.zeros((2, 4, 2, rows, width // 2), BF16)
    for pieces, place in (((near, *near_got), zh), ((away, *away_got), far_zh)):
        for by, piece in zip((0, 3, 1, 2), pieces):
            full = put(full, piece, place, x_to[by])
    full = full.reshape(features, -1)
    back = jnp.concatenate(
        [
            half
            for block in (near_own[rows:], backs[0], near_other[rows:], swapped(backs[1], "core"))
            for half in split_pair(block)
        ],
        axis=0,
    )

    product = lax.dot_general(
        normed, full, (((0,), (0,)), ((), ())), preferred_element_type=F32
    )
    gate, up = split_pair(product)
    d_gate, d_up = derivatives(gate, up, back.astype(F32))
    d_gate, d_up = d_gate.astype(BF16), d_up.astype(BF16)
    row_part = jnp.sum(d_gate.astype(F32) * gate + d_up.astype(F32) * up, axis=1)
    d_both = join_pair(d_gate, d_up)

    def d_normed(d):
        return lax.dot_general(full, d, (((1,), (1,)), ((), ())), preferred_element_type=F32)

    by_rows = normed.reshape(2, 4, 2 * rows, 4 * group)

    def part(zplace, xplace):
        return jnp.dot(as_block(by_rows, zplace, xplace), d_both, preferred_element_type=F32)

    away_parts = [part(far_zh, x_to[by]).astype(BF16) for by in steps]
    near_parts = [part(zh, x_to[by]).astype(BF16) for by in steps]
    away_got = [turned(away_parts[k], "x", steps[k]) for k in (0, 1)]

    got = swapped(d_normed(d_both[2 * group :]).astype(BF16), "core")
    row = row_part[: 2 * group] + swapped(row_part[2 * group :], "core")
    mine = d_normed(d_both[: 2 * group]) + got.astype(F32)
    mine = mine.reshape(4, 4, own_rows, 2 * group)

    def section(index):
        zero = jnp.uint32(0)
        block = lax.dynamic_slice(
            mine, (zero, index, zero, zero), (4, 1, own_rows, 2 * group)
        )
        return block.reshape(4 * own_rows, 2 * group)

    sends = [with_rows(section(sec_to[by]), row) for by in steps]
    *away_got, away_parts[2], sends[0], sends[1], sends[2] = barrier(
        (*away_got, away_parts[2], *sends)
    )
    away_got.append(turned(away_parts[2], "x", 2))
    got = [turned(s, "sec", by) for s, by in zip(sends, steps)]
    away_got[2], *near_parts = barrier((away_got[2], *near_parts))
    near_got = [turned(p, "x", by) for p, by in zip(near_parts, steps)]
    g_away = part(far_zh, x) + sum(g.astype(F32) for g in away_got)
    g_away = g_away.astype(BF16).reshape(2, rows, -1)
    late = {}
    g_away, late[1], late[3], late[2] = barrier((g_away, *(tp_to[by] for by in steps)))
    away_keep = swapped(as_block(g_away, core), "zh")
    away_give = swapped(as_block(g_away, other_core), "zh")

    total = section(sec) + sum(block_of(g) for g in got)
    row = row + sum(row_of(g) for g in got)
    mine = total.reshape(4, own_rows, 2 * group)
    sends = [with_rows(as_block(mine, late[by]), row) for by in steps]
    got = [turned(s, "tp", by) for s, by in zip(sends, steps)]
    total = as_block(mine, tp) + sum(block_of(g) for g in got)
    row = row + sum(row_of(g) for g in got)

    own_inputs = lax.dynamic_slice(inputs, (offset, jnp.uint32(0)), (own_rows, 2 * group))
    own_inputs = own_inputs.astype(F32)
    own_gain = lax.dynamic_slice(norm_gain, (offset,), (own_rows,))[:, None]
    gain_part = jnp.sum(total * own_inputs * inv_rms, axis=1)
    gain_rows = jnp.pad(gain_part, (0, 2 * group - own_rows)).reshape(2, group)
    send = with_rows(total[:, group:], row[group:], gain_rows[0], gain_rows[1])
    send, near_got[0], near_got[1], late_zh = barrier((send, near_got[0], near_got[1], zh))
    got = swapped(send, "zh")
    g_near = part(late_zh, x) + sum(g.astype(F32) for g in near_got)
    g_near = g_near.astype(BF16).reshape(2, rows, -1)
    give = swapped(jnp.stack([as_block(g_near, other_core), away_give]), "core")
    grad_gain = gain_part + jnp.concatenate([row_of(got, 1), row_of(got, 2)])[:own_rows]
    grad_gain = grad_gain + swapped(grad_gain, "core")
    grad_gain = grad_gain + sum(turned(grad_gain, "x", by) for by in steps)
    d_own, row_sum = total[:, :group] + block_of(got), row[:group] + row_of(got)
    inv = inv_rms[:group]
    own_inputs = own_inputs[:, :group]
    grad_tokens = inv * own_gain * d_own - own_inputs * (inv**2 * row_sum / features)
    grad_gate, grad_up = joined(g_near, away_keep, give)
    return grad_tokens.T.astype(BF16), grad_gain, grad_gate, grad_up


def solution(mesh):
    split = Mesh(
        mesh.devices.reshape(2, 4, 2, mesh.shape["tp"], mesh.shape["section"]),
        (*DP, *COLS),
    )
    weights = P(DP, COLS)
    return jax.shard_map(
        shards,
        mesh=split,
        in_specs=(P(DP, "sec"), weights, P(), weights, weights),
        out_specs=(weights, P(COLS), weights, weights),
        check_vma=False,
    )
```

```python
import functools

import jax
import jax.numpy as jnp
from jax import lax
from jax.experimental import pallas as pl
from jax.experimental.pallas import tpu as pltpu
from jax.sharding import Mesh
from jax.sharding import PartitionSpec as P

DP = ("zh", "x", "core")
COLS = ("tp", "sec")
EPS = 1e-06
LANES = 128
EXTRA = 16
F32 = jnp.float32
BF16 = jnp.bfloat16
SDS = jax.ShapeDtypeStruct


def turned(array, axis, by):
    n = lax.axis_size(axis)
    return lax.ppermute(array, axis, [(i, (i + by) % n) for i in range(n)])


def swapped(array, axis):
    return turned(array, axis, 1)


def unsigned(index):
    return index.astype(jnp.uint32)


def as_block(array, *lead):
    n = len(lead)
    zeros = [jnp.uint32(0)] * (array.ndim - n)
    part = lax.dynamic_slice(array, (*lead, *zeros), (*([1] * n), *array.shape[n:]))
    return part.reshape(array.shape[n:])


def put(array, part, *lead):
    zeros = [jnp.uint32(0)] * (array.ndim - len(lead))
    part = part.reshape(*([1] * len(lead)), *array.shape[len(lead) :])
    return lax.dynamic_update_slice(array, part, (*lead, *zeros))


def parts_of(width):
    main = width // LANES // 4 * LANES
    rest = width // 4 - main
    return main, rest


def pack_kernel(main, rest, aways, gate_ref, up_ref, back_ref, *outs):
    half = back_ref.shape[0] // 2
    zh, core = lax.axis_index("zh"), lax.axis_index("core")
    rows = gate_ref.shape[0]
    if aways:
        weights, backs = outs[:2], [outs[2].at[0], outs[2].at[1]]
    else:
        weights = [out.at[pl.ds(0, rows)] for out in outs]
        backs = [out.at[pl.ds(rows, half)] for out in outs]
    sources = (
        (weights, gate_ref, up_ref),
        (backs, back_ref.at[pl.ds(0, half)], back_ref.at[pl.ds(half, half)]),
    )
    for other in range(2):
        q = (zh ^ aways) * 2 + (core ^ other)
        wide = pl.ds(pl.multiple_of(q * main, LANES), main)
        for targets, first, second in sources:
            out = targets[other]
            out[:, pl.ds(0, main)] = first[:, wide]
            out[:, pl.ds(main, main)] = second[:, wide]
            thin = []
            for ref in (first, second):
                tail = ref[:, pl.ds(4 * main, 4 * rest)]
                pick = tail[:, :rest]
                for k in range(1, 4):
                    pick = jnp.where(q == k, tail[:, k * rest : (k + 1) * rest], pick)
                thin.append(pick)
            out[:, pl.ds(2 * main, 2 * rest)] = jnp.concatenate(thin, axis=1)


def packed(aways, w_gate, w_up, hidden_grad):
    rows, width = w_gate.shape
    main, rest = parts_of(width)
    half = hidden_grad.shape[0] // 2
    if aways:
        outs = [(rows, width // 2), (rows, width // 2), (2, half, width // 2)]
    else:
        outs = [(rows + half, width // 2)] * 2
    return pl.pallas_call(
        functools.partial(pack_kernel, main, rest, aways),
        out_shape=[pltpu.VMEM(shape, BF16) for shape in outs],
        in_specs=[pl.BlockSpec(memory_space=pltpu.VMEM)] * 3,
        out_specs=[pl.BlockSpec(memory_space=pltpu.VMEM)] * len(outs),
        name="pack",
    )(w_gate, w_up, hidden_grad)


def join_kernel(main, rest, near_ref, keep_ref, give_ref, gate_ref, up_ref):
    zh, core = lax.axis_index("zh"), lax.axis_index("core")
    tails = [[None] * 4, [None] * 4]
    for aways in range(2):
        for other in range(2):
            ref = give_ref.at[aways] if other else keep_ref if aways else near_ref.at[core]
            q = (zh ^ aways) * 2 + (core ^ other)
            wide = pl.ds(pl.multiple_of(q * main, LANES), main)
            gate_ref[:, wide] = ref[:, pl.ds(0, main)]
            up_ref[:, wide] = ref[:, pl.ds(main, main)]
            tail = ref[:, pl.ds(2 * main, 2 * rest)]
            for i in range(2):
                thin = tail[:, i * rest : (i + 1) * rest]
                for k in range(4):
                    old = tails[i][k]
                    tails[i][k] = thin if old is None else jnp.where(q == k, thin, old)
    gate_ref[:, pl.ds(4 * main, 4 * rest)] = jnp.concatenate(tails[0], axis=1)
    up_ref[:, pl.ds(4 * main, 4 * rest)] = jnp.concatenate(tails[1], axis=1)


def joined(near, keep, give):
    rows, half = keep.shape
    main, rest = parts_of(half * 2)
    out = SDS((rows, half * 2), BF16)
    return pl.pallas_call(
        functools.partial(join_kernel, main, rest),
        out_shape=(out, out),
        in_specs=[pl.BlockSpec(memory_space=pltpu.VMEM)] * 3,
        out_specs=(pl.BlockSpec(memory_space=pltpu.VMEM),) * 2,
        name="join",
    )(near, keep, give)


def split_pair(block):
    main, rest = parts_of(block.shape[1] * 2)
    first = jnp.concatenate([block[:, :main], block[:, 2 * main : 2 * main + rest]], axis=1)
    second = jnp.concatenate([block[:, main : 2 * main], block[:, 2 * main + rest :]], axis=1)
    return first, second


def join_pair(first, second):
    main, rest = parts_of(first.shape[1] * 4)
    return jnp.concatenate(
        [first[:, :main], second[:, :main], first[:, main:], second[:, main:]], axis=1
    )


def ordered(own, other, first):
    return jnp.where(first, jnp.stack([own, other]), jnp.stack([other, own]))


def halves(row):
    high = row.astype(BF16)
    return high, (row - high.astype(F32)).astype(BF16)


def with_rows(block, *rows):
    shape = (EXTRA, block.shape[1])
    which = lax.broadcasted_iota(jnp.int32, shape, 0)
    tail = jnp.zeros(shape, BF16)
    for k, half in enumerate([half for row in rows for half in halves(row)]):
        tail = jnp.where(which == k, half[None, :], tail)
    return jnp.concatenate([block.astype(BF16), tail], axis=0)


def row_of(packed_rows, k=0):
    at_row = packed_rows.shape[0] - EXTRA + 2 * k
    return packed_rows[at_row].astype(F32) + packed_rows[at_row + 1].astype(F32)


def block_of(packed_rows):
    return packed_rows[: packed_rows.shape[0] - EXTRA].astype(F32)


def derivatives(gate, up, back):
    hidden, pull = jax.vjp(lambda g, u: jax.nn.gelu(g, approximate=True) * u, gate, up)
    return pull(back)


def shards(tokens, hidden_grad, norm_gain, w_gate, w_up):
    rows, width = w_gate.shape
    group = tokens.shape[0]
    features = norm_gain.shape[0]
    own_rows = features // 16
    barrier = lax.optimization_barrier

    zh, x, core, tp, sec = (unsigned(lax.axis_index(a)) for a in (*DP, *COLS))
    steps = (1, 3, 2)
    far_zh, other_core = 1 - zh, 1 - core
    first_core = core == 0
    x_to = {by: (x + by) & 3 for by in range(4)}
    sec_to = {by: (sec + by) & 3 for by in range(4)}
    tp_to = {by: (tp + by) & 3 for by in range(4)}
    offset = (tp * 4 + sec) * own_rows

    own_t = tokens.T
    far_t = swapped(own_t, "zh")

    near_own, near_other = packed(0, w_gate, w_up, hidden_grad)
    hidden_grad, near_own = barrier((hidden_grad, near_own))
    away_own, away_other, backs = packed(1, w_gate, w_up, hidden_grad)
    near_other = swapped(near_other, "core")
    away_other, far_t = barrier((away_other, far_t))
    away_own, away_other = swapped(away_own, "zh"), swapped(away_other, "zh")

    near = ordered(near_own[:rows], near_other[:rows], first_core)
    near, own_t = barrier((near, own_t))
    near_got = [turned(near, "x", by) for by in steps]

    both = jnp.concatenate([own_t, far_t], axis=1)
    copies = jnp.broadcast_to(both, (4, *both.shape))
    inputs = lax.all_to_all(copies, "sec", 0, 0, tiled=True)

    near_got[0], near_got[1], backs, late_first = barrier(
        (near_got[0], near_got[1], backs, first_core)
    )
    away_other = swapped(away_other, "core")
    backs = swapped(backs, "zh")
    away = ordered(away_own, away_other, late_first)
    away_got = [turned(away, "x", by) for by in steps]
    inputs = inputs.reshape(features, 2 * group)
    wide = inputs.astype(F32)
    inv_rms = lax.rsqrt(jnp.mean(wide * wide, axis=0) + EPS)
    normed = (wide * inv_rms * norm_gain[:, None]).astype(BF16)
    normed, away_got[0] = barrier((normed, away_got[0]))
    normed = jnp.concatenate([normed, swapped(normed, "core")], axis=1)

    backs, *away_got = barrier((backs, *away_got))
    full = jnp.zeros((2, 4, 2, rows, width // 2), BF16)
    for pieces, place in (((near, *near_got), zh), ((away, *away_got), far_zh)):
        for by, piece in zip((0, 3, 1, 2), pieces):
            full = put(full, piece, place, x_to[by])
    full = full.reshape(features, -1)
    back = jnp.concatenate(
        [
            half
            for block in (near_own[rows:], backs[0], near_other[rows:], swapped(backs[1], "core"))
            for half in split_pair(block)
        ],
        axis=0,
    )

    product = lax.dot_general(
        normed, full, (((0,), (0,)), ((), ())), preferred_element_type=F32
    )
    gate, up = split_pair(product)
    d_gate, d_up = derivatives(gate, up, back.astype(F32))
    d_gate, d_up = d_gate.astype(BF16), d_up.astype(BF16)
    row_part = jnp.sum(d_gate.astype(F32) * gate + d_up.astype(F32) * up, axis=1)
    d_both = join_pair(d_gate, d_up)

    def d_normed(d):
        return lax.dot_general(full, d, (((1,), (1,)), ((), ())), preferred_element_type=F32)

    by_rows = normed.reshape(2, 4, 2 * rows, 4 * group)

    def parts(zplace):
        mine = as_block(by_rows, zplace)
        out = [jnp.dot(mine[k], d_both, preferred_element_type=F32) for k in range(4)]
        return jnp.stack([o.astype(BF16) for o in out])

    def summed(parts_of_x):
        got = lax.all_to_all(parts_of_x, "x", 0, 0, tiled=True)
        return sum(got[k].astype(F32) for k in range(4)).astype(BF16)

    away_parts, near_parts = parts(far_zh), parts(zh)

    theirs = d_normed(d_both[2 * group :]).astype(BF16)
    theirs, away_parts = barrier((theirs, away_parts))
    got = swapped(theirs, "core")
    g_away = summed(away_parts)
    row = row_part[: 2 * group] + swapped(row_part[2 * group :], "core")
    mine = d_normed(d_both[: 2 * group]) + got.astype(F32)
    mine = mine.reshape(4, 4, own_rows, 2 * group)

    def section(index):
        zero = jnp.uint32(0)
        block = lax.dynamic_slice(
            mine, (zero, index, zero, zero), (4, 1, own_rows, 2 * group)
        )
        return block.reshape(4 * own_rows, 2 * group)

    sends = [with_rows(section(sec_to[by]), row) for by in steps]
    g_away, near_parts, *sends = barrier((g_away, near_parts, *sends))
    got = [turned(s, "sec", by) for s, by in zip(sends, steps)]
    g_away = g_away.reshape(2, rows, -1)
    late = {}
    g_near, late[1], late[3], late[2] = barrier(
        (summed(near_parts), *(tp_to[by] for by in steps))
    )
    g_near = g_near.reshape(2, rows, -1)
    away_keep = swapped(as_block(g_away, core), "zh")
    away_give = swapped(as_block(g_away, other_core), "zh")

    total = section(sec) + sum(block_of(g) for g in got)
    row = row + sum(row_of(g) for g in got)
    mine = total.reshape(4, own_rows, 2 * group)
    sends = [with_rows(as_block(mine, late[by]), row) for by in steps]
    got = [turned(s, "tp", by) for s, by in zip(sends, steps)]
    total = as_block(mine, tp) + sum(block_of(g) for g in got)
    row = row + sum(row_of(g) for g in got)

    own_inputs = lax.dynamic_slice(inputs, (offset, jnp.uint32(0)), (own_rows, 2 * group))
    own_inputs = own_inputs.astype(F32)
    own_gain = lax.dynamic_slice(norm_gain, (offset,), (own_rows,))[:, None]
    gain_part = jnp.sum(total * own_inputs * inv_rms, axis=1)
    gain_rows = jnp.pad(gain_part, (0, 2 * group - own_rows)).reshape(2, group)
    send = with_rows(total[:, group:], row[group:], gain_rows[0], gain_rows[1])
    send, away_give = barrier((send, away_give))
    got = swapped(send, "zh")
    give = swapped(jnp.stack([as_block(g_near, other_core), away_give]), "core")
    grad_gain = gain_part + jnp.concatenate([row_of(got, 1), row_of(got, 2)])[:own_rows]
    grad_gain = grad_gain + swapped(grad_gain, "core")
    grad_gain = grad_gain + sum(turned(grad_gain, "x", by) for by in steps)
    d_own, row_sum = total[:, :group] + block_of(got), row[:group] + row_of(got)
    inv = inv_rms[:group]
    own_inputs = own_inputs[:, :group]
    grad_tokens = inv * own_gain * d_own - own_inputs * (inv**2 * row_sum / features)
    grad_gate, grad_up = joined(g_near, away_keep, give)
    return grad_tokens.T.astype(BF16), grad_gain, grad_gate, grad_up


def solution(mesh):
    split = Mesh(
        mesh.devices.reshape(2, 4, 2, mesh.shape["tp"], mesh.shape["section"]),
        (*DP, *COLS),
    )
    weights = P(DP, COLS)
    return jax.shard_map(
        shards,
        mesh=split,
        in_specs=(P(DP, "sec"), weights, P(), weights, weights),
        out_specs=(weights, P(COLS), weights, weights),
        check_vma=False,
    )
```

```python
import functools

import jax
import jax.numpy as jnp
from jax import lax
from jax.experimental import pallas as pl
from jax.experimental.pallas import tpu as pltpu
from jax.sharding import Mesh
from jax.sharding import PartitionSpec as P

DP = ("zh", "x", "core")
COLS = ("tp", "sec")
EPS = 1e-06
LANES = 128
EXTRA = 16
F32 = jnp.float32
BF16 = jnp.bfloat16
SDS = jax.ShapeDtypeStruct


def turned(array, axis, by):
    n = lax.axis_size(axis)
    return lax.ppermute(array, axis, [(i, (i + by) % n) for i in range(n)])


def swapped(array, axis):
    return turned(array, axis, 1)


def unsigned(index):
    return index.astype(jnp.uint32)


def as_block(array, *lead):
    n = len(lead)
    zeros = [jnp.uint32(0)] * (array.ndim - n)
    part = lax.dynamic_slice(array, (*lead, *zeros), (*([1] * n), *array.shape[n:]))
    return part.reshape(array.shape[n:])


def put(array, part, *lead):
    zeros = [jnp.uint32(0)] * (array.ndim - len(lead))
    part = part.reshape(*([1] * len(lead)), *array.shape[len(lead) :])
    return lax.dynamic_update_slice(array, part, (*lead, *zeros))


def parts_of(width):
    main = width // LANES // 4 * LANES
    rest = width // 4 - main
    return main, rest


def pack_kernel(main, rest, aways, gate_ref, up_ref, back_ref, *outs):
    half = back_ref.shape[0] // 2
    zh, core = lax.axis_index("zh"), lax.axis_index("core")
    rows = gate_ref.shape[0]
    if aways:
        weights, backs = [[out.at[0], out.at[1]] for out in outs]
    else:
        weights = [out.at[pl.ds(0, rows)] for out in outs]
        backs = [out.at[pl.ds(rows, half)] for out in outs]
    sources = (
        (weights, gate_ref, up_ref),
        (backs, back_ref.at[pl.ds(0, half)], back_ref.at[pl.ds(half, half)]),
    )
    for other in range(2):
        q = (zh ^ aways) * 2 + (core ^ other)
        wide = pl.ds(pl.multiple_of(q * main, LANES), main)
        for targets, first, second in sources:
            out = targets[other]
            out[:, pl.ds(0, main)] = first[:, wide]
            out[:, pl.ds(main, main)] = second[:, wide]
            thin = []
            for ref in (first, second):
                tail = ref[:, pl.ds(4 * main, 4 * rest)]
                pick = tail[:, :rest]
                for k in range(1, 4):
                    pick = jnp.where(q == k, tail[:, k * rest : (k + 1) * rest], pick)
                thin.append(pick)
            out[:, pl.ds(2 * main, 2 * rest)] = jnp.concatenate(thin, axis=1)


def packed(aways, w_gate, w_up, hidden_grad):
    rows, width = w_gate.shape
    main, rest = parts_of(width)
    half = hidden_grad.shape[0] // 2
    if aways:
        outs = [(2, rows, width // 2), (2, half, width // 2)]
    else:
        outs = [(rows + half, width // 2)] * 2
    return pl.pallas_call(
        functools.partial(pack_kernel, main, rest, aways),
        out_shape=[pltpu.VMEM(shape, BF16) for shape in outs],
        in_specs=[pl.BlockSpec(memory_space=pltpu.VMEM)] * 3,
        out_specs=[pl.BlockSpec(memory_space=pltpu.VMEM)] * len(outs),
        name="pack",
    )(w_gate, w_up, hidden_grad)


def join_kernel(main, rest, near_ref, keep_ref, give_ref, gate_ref, up_ref):
    zh, core = lax.axis_index("zh"), lax.axis_index("core")
    tails = [[None] * 4, [None] * 4]
    for aways in range(2):
        for other in range(2):
            ref = give_ref.at[aways] if other else keep_ref if aways else near_ref.at[core]
            q = (zh ^ aways) * 2 + (core ^ other)
            wide = pl.ds(pl.multiple_of(q * main, LANES), main)
            gate_ref[:, wide] = ref[:, pl.ds(0, main)]
            up_ref[:, wide] = ref[:, pl.ds(main, main)]
            tail = ref[:, pl.ds(2 * main, 2 * rest)]
            for i in range(2):
                thin = tail[:, i * rest : (i + 1) * rest]
                for k in range(4):
                    old = tails[i][k]
                    tails[i][k] = thin if old is None else jnp.where(q == k, thin, old)
    gate_ref[:, pl.ds(4 * main, 4 * rest)] = jnp.concatenate(tails[0], axis=1)
    up_ref[:, pl.ds(4 * main, 4 * rest)] = jnp.concatenate(tails[1], axis=1)


def joined(near, keep, give):
    rows, half = keep.shape
    main, rest = parts_of(half * 2)
    out = SDS((rows, half * 2), BF16)
    return pl.pallas_call(
        functools.partial(join_kernel, main, rest),
        out_shape=(out, out),
        in_specs=[pl.BlockSpec(memory_space=pltpu.VMEM)] * 3,
        out_specs=(pl.BlockSpec(memory_space=pltpu.VMEM),) * 2,
        name="join",
    )(near, keep, give)


def split_pair(block):
    main, rest = parts_of(block.shape[1] * 2)
    first = jnp.concatenate([block[:, :main], block[:, 2 * main : 2 * main + rest]], axis=1)
    second = jnp.concatenate([block[:, main : 2 * main], block[:, 2 * main + rest :]], axis=1)
    return first, second


def join_pair(first, second):
    main, rest = parts_of(first.shape[1] * 4)
    return jnp.concatenate(
        [first[:, :main], second[:, :main], first[:, main:], second[:, main:]], axis=1
    )


def ordered(own, other, first):
    return jnp.where(first, jnp.stack([own, other]), jnp.stack([other, own]))


def halves(row):
    high = row.astype(BF16)
    return high, (row - high.astype(F32)).astype(BF16)


def with_rows(block, *rows):
    shape = (EXTRA, block.shape[1])
    which = lax.broadcasted_iota(jnp.int32, shape, 0)
    tail = jnp.zeros(shape, BF16)
    for k, half in enumerate([half for row in rows for half in halves(row)]):
        tail = jnp.where(which == k, half[None, :], tail)
    return jnp.concatenate([block.astype(BF16), tail], axis=0)


def row_of(packed_rows, k=0):
    at_row = packed_rows.shape[0] - EXTRA + 2 * k
    return packed_rows[at_row].astype(F32) + packed_rows[at_row + 1].astype(F32)


def block_of(packed_rows):
    return packed_rows[: packed_rows.shape[0] - EXTRA].astype(F32)


def derivatives(gate, up, back):
    hidden, pull = jax.vjp(lambda g, u: jax.nn.gelu(g, approximate=True) * u, gate, up)
    return pull(back)


def shards(tokens, hidden_grad, norm_gain, w_gate, w_up):
    rows, width = w_gate.shape
    group = tokens.shape[0]
    features = norm_gain.shape[0]
    own_rows = features // 16
    barrier = lax.optimization_barrier

    zh, x, core, tp, sec = (unsigned(lax.axis_index(a)) for a in (*DP, *COLS))
    steps = (1, 3, 2)
    far_zh, other_core = 1 - zh, 1 - core
    first_core = core == 0
    x_to = {by: (x + by) & 3 for by in range(4)}
    sec_to = {by: (sec + by) & 3 for by in range(4)}
    tp_to = {by: (tp + by) & 3 for by in range(4)}
    offset = (tp * 4 + sec) * own_rows

    own_t = tokens.T
    far_t = swapped(own_t, "zh")

    near_own, near_other = packed(0, w_gate, w_up, hidden_grad)
    hidden_grad, near_own = barrier((hidden_grad, near_own))
    away, backs = packed(1, w_gate, w_up, hidden_grad)
    near_other = swapped(near_other, "core")
    away = swapped(away, "zh")

    near = ordered(near_own[:rows], near_other[:rows], first_core)
    near, own_t = barrier((near, own_t))
    near_got = [turned(near, "x", by) for by in steps]

    both = jnp.concatenate([own_t, far_t], axis=1)
    section_got = [turned(both, "sec", by) for by in steps]

    near_got[0], near_got[1], backs, late_first = barrier(
        (near_got[0], near_got[1], backs, first_core)
    )
    away_own, away_other = away[0], swapped(away[1], "core")
    backs = swapped(backs, "zh")
    away = ordered(away_own, away_other, late_first)
    late = {}
    away, late[0], late[1], late[2], late[3] = barrier((away, *(sec_to[by] for by in range(4))))
    away_got = [turned(away, "x", by) for by in steps]

    inputs = jnp.zeros((4, *both.shape), BF16)
    for by, piece in zip((0, 3, 1, 2), (both, *section_got)):
        inputs = put(inputs, piece, late[by])
    inputs = inputs.reshape(features, 2 * group)
    wide = inputs.astype(F32)
    inv_rms = lax.rsqrt(jnp.mean(wide * wide, axis=0) + EPS)
    normed = (wide * inv_rms * norm_gain[:, None]).astype(BF16)
    normed, away_got[0] = barrier((normed, away_got[0]))
    normed_other, away_got[2] = barrier((swapped(normed, "core"), away_got[2]))
    normed = jnp.concatenate([normed, normed_other], axis=1)

    backs, *away_got = barrier((backs, *away_got))
    full = jnp.zeros((2, 4, 2, rows, width // 2), BF16)
    for pieces, place in (((near, *near_got), zh), ((away, *away_got), far_zh)):
        for by, piece in zip((0, 3, 1, 2), pieces):
            full = put(full, piece, place, x_to[by])
    full = full.reshape(features, -1)
    back = jnp.concatenate(
        [
            half
            for block in (near_own[rows:], backs[0], near_other[rows:], swapped(backs[1], "core"))
            for half in split_pair(block)
        ],
        axis=0,
    )

    product = lax.dot_general(
        normed, full, (((0,), (0,)), ((), ())), preferred_element_type=F32
    )
    gate, up = split_pair(product)
    d_gate, d_up = derivatives(gate, up, back.astype(F32))
    d_gate, d_up = d_gate.astype(BF16), d_up.astype(BF16)
    row_part = jnp.sum(d_gate.astype(F32) * gate + d_up.astype(F32) * up, axis=1)
    d_both = join_pair(d_gate, d_up)

    def d_normed(d):
        return lax.dot_general(full, d, (((1,), (1,)), ((), ())), preferred_element_type=F32)

    by_rows = normed.reshape(2, 4, 2 * rows, 4 * group)

    def part(zplace, xplace):
        return jnp.dot(as_block(by_rows, zplace, xplace), d_both, preferred_element_type=F32)

    away_parts = [part(far_zh, x_to[by]).astype(BF16) for by in steps]
    near_parts = [part(zh, x_to[by]).astype(BF16) for by in steps]
    away_got = [turned(away_parts[k], "x", steps[k]) for k in (0, 1)]

    got = swapped(d_normed(d_both[2 * group :]).astype(BF16), "core")
    row = row_part[: 2 * group] + swapped(row_part[2 * group :], "core")
    mine = d_normed(d_both[: 2 * group]) + got.astype(F32)
    mine = mine.reshape(4, 4, own_rows, 2 * group)

    def section(index):
        zero = jnp.uint32(0)
        block = lax.dynamic_slice(
            mine, (zero, index, zero, zero), (4, 1, own_rows, 2 * group)
        )
        return block.reshape(4 * own_rows, 2 * group)

    sends = [with_rows(section(sec_to[by]), row) for by in steps]
    *away_got, away_parts[2], sends[0], sends[1], sends[2] = barrier(
        (*away_got, away_parts[2], *sends)
    )
    away_got.append(turned(away_parts[2], "x", 2))
    got = [turned(s, "sec", by) for s, by in zip(sends, steps)]
    away_got[2], *near_parts = barrier((away_got[2], *near_parts))
    near_got = [turned(p, "x", by) for p, by in zip(near_parts, steps)]
    g_away = part(far_zh, x) + sum(g.astype(F32) for g in away_got)
    g_away = g_away.astype(BF16).reshape(2, rows, -1)
    late = {}
    g_away, late[1], late[3], late[2] = barrier((g_away, *(tp_to[by] for by in steps)))
    away_keep = swapped(as_block(g_away, core), "zh")
    away_give = swapped(as_block(g_away, other_core), "zh")

    total = section(sec) + sum(block_of(g) for g in got)
    row = row + sum(row_of(g) for g in got)
    mine = total.reshape(4, own_rows, 2 * group)
    sends = [with_rows(as_block(mine, late[by]), row) for by in steps]
    got = [turned(s, "tp", by) for s, by in zip(sends, steps)]
    total = as_block(mine, tp) + sum(block_of(g) for g in got)
    row = row + sum(row_of(g) for g in got)

    own_inputs = lax.dynamic_slice(inputs, (offset, jnp.uint32(0)), (own_rows, 2 * group))
    own_inputs = own_inputs.astype(F32)
    own_gain = lax.dynamic_slice(norm_gain, (offset,), (own_rows,))[:, None]
    gain_part = jnp.sum(total * own_inputs * inv_rms, axis=1)
    gain_rows = jnp.pad(gain_part, (0, 2 * group - own_rows)).reshape(2, group)
    send = with_rows(total[:, group:], row[group:], gain_rows[0], gain_rows[1])
    send, near_got[0], near_got[1], late_zh = barrier((send, near_got[0], near_got[1], zh))
    got = swapped(send, "zh")
    g_near = part(late_zh, x) + sum(g.astype(F32) for g in near_got)
    g_near = g_near.astype(BF16).reshape(2, rows, -1)
    give = swapped(jnp.stack([as_block(g_near, other_core), away_give]), "core")
    grad_gain = gain_part + jnp.concatenate([row_of(got, 1), row_of(got, 2)])[:own_rows]
    grad_gain = grad_gain + swapped(grad_gain, "core")
    grad_gain = grad_gain + sum(turned(grad_gain, "x", by) for by in steps)
    d_own, row_sum = total[:, :group] + block_of(got), row[:group] + row_of(got)
    inv = inv_rms[:group]
    own_inputs = own_inputs[:, :group]
    grad_tokens = inv * own_gain * d_own - own_inputs * (inv**2 * row_sum / features)
    grad_gate, grad_up = joined(g_near, away_keep, give)
    return grad_tokens.T.astype(BF16), grad_gain, grad_gate, grad_up


def solution(mesh):
    split = Mesh(
        mesh.devices.reshape(2, 4, 2, mesh.shape["tp"], mesh.shape["section"]),
        (*DP, *COLS),
    )
    weights = P(DP, COLS)
    return jax.shard_map(
        shards,
        mesh=split,
        in_specs=(P(DP, "sec"), weights, P(), weights, weights),
        out_specs=(weights, P(COLS), weights, weights),
        check_vma=False,
    )
```

```python
import functools

import jax
import jax.numpy as jnp
from jax import lax
from jax.experimental import pallas as pl
from jax.experimental.pallas import tpu as pltpu
from jax.sharding import Mesh
from jax.sharding import PartitionSpec as P

DP = ("zh", "x", "core")
COLS = ("tp", "sec")
EPS = 1e-06
LANES = 128
EXTRA = 16
F32 = jnp.float32
BF16 = jnp.bfloat16
SDS = jax.ShapeDtypeStruct


def turned(array, axis, by):
    n = lax.axis_size(axis)
    return lax.ppermute(array, axis, [(i, (i + by) % n) for i in range(n)])


def swapped(array, axis):
    return turned(array, axis, 1)


def unsigned(index):
    return index.astype(jnp.uint32)


def as_block(array, *lead):
    n = len(lead)
    zeros = [jnp.uint32(0)] * (array.ndim - n)
    part = lax.dynamic_slice(array, (*lead, *zeros), (*([1] * n), *array.shape[n:]))
    return part.reshape(array.shape[n:])


def put(array, part, *lead):
    zeros = [jnp.uint32(0)] * (array.ndim - len(lead))
    part = part.reshape(*([1] * len(lead)), *array.shape[len(lead) :])
    return lax.dynamic_update_slice(array, part, (*lead, *zeros))


def parts_of(width):
    main = width // LANES // 4 * LANES
    rest = width // 4 - main
    return main, rest


def pack_kernel(main, rest, aways, gate_ref, up_ref, back_ref, *outs):
    half = back_ref.shape[0] // 2
    zh, core = lax.axis_index("zh"), lax.axis_index("core")
    rows = gate_ref.shape[0]
    if aways:
        weights, backs = outs[:2], [outs[2].at[0], outs[2].at[1]]
    else:
        weights = [out.at[pl.ds(0, rows)] for out in outs]
        backs = [out.at[pl.ds(rows, half)] for out in outs]
    sources = (
        (weights, gate_ref, up_ref),
        (backs, back_ref.at[pl.ds(0, half)], back_ref.at[pl.ds(half, half)]),
    )
    for other in range(2):
        q = (zh ^ aways) * 2 + (core ^ other)
        wide = pl.ds(pl.multiple_of(q * main, LANES), main)
        for targets, first, second in sources:
            out = targets[other]
            out[:, pl.ds(0, main)] = first[:, wide]
            out[:, pl.ds(main, main)] = second[:, wide]
            thin = []
            for ref in (first, second):
                tail = ref[:, pl.ds(4 * main, 4 * rest)]
                turn = pltpu.roll(tail.astype(F32), ((4 - q) & 3) * rest, 1)
                thin.append(turn[:, :rest].astype(BF16))
            out[:, pl.ds(2 * main, 2 * rest)] = jnp.concatenate(thin, axis=1)


def packed(aways, w_gate, w_up, hidden_grad):
    rows, width = w_gate.shape
    main, rest = parts_of(width)
    half = hidden_grad.shape[0] // 2
    if aways:
        outs = [(rows, width // 2), (rows, width // 2), (2, half, width // 2)]
    else:
        outs = [(rows + half, width // 2)] * 2
    return pl.pallas_call(
        functools.partial(pack_kernel, main, rest, aways),
        out_shape=[pltpu.VMEM(shape, BF16) for shape in outs],
        in_specs=[pl.BlockSpec(memory_space=pltpu.VMEM)] * 3,
        out_specs=[pl.BlockSpec(memory_space=pltpu.VMEM)] * len(outs),
        name="pack",
    )(w_gate, w_up, hidden_grad)


def join_kernel(main, rest, near_ref, keep_ref, give_ref, gate_ref, up_ref):
    zh, core = lax.axis_index("zh"), lax.axis_index("core")
    tails = [[None] * 4, [None] * 4]
    for aways in range(2):
        for other in range(2):
            ref = give_ref.at[aways] if other else keep_ref if aways else near_ref.at[core]
            q = (zh ^ aways) * 2 + (core ^ other)
            wide = pl.ds(pl.multiple_of(q * main, LANES), main)
            gate_ref[:, wide] = ref[:, pl.ds(0, main)]
            up_ref[:, wide] = ref[:, pl.ds(main, main)]
            tail = ref[:, pl.ds(2 * main, 2 * rest)]
            for i in range(2):
                thin = tail[:, i * rest : (i + 1) * rest]
                for k in range(4):
                    old = tails[i][k]
                    tails[i][k] = thin if old is None else jnp.where(q == k, thin, old)
    gate_ref[:, pl.ds(4 * main, 4 * rest)] = jnp.concatenate(tails[0], axis=1)
    up_ref[:, pl.ds(4 * main, 4 * rest)] = jnp.concatenate(tails[1], axis=1)


def joined(near, keep, give):
    rows, half = keep.shape
    main, rest = parts_of(half * 2)
    out = SDS((rows, half * 2), BF16)
    return pl.pallas_call(
        functools.partial(join_kernel, main, rest),
        out_shape=(out, out),
        in_specs=[pl.BlockSpec(memory_space=pltpu.VMEM)] * 3,
        out_specs=(pl.BlockSpec(memory_space=pltpu.VMEM),) * 2,
        name="join",
    )(near, keep, give)


def split_pair(block):
    main, rest = parts_of(block.shape[1] * 2)
    first = jnp.concatenate([block[:, :main], block[:, 2 * main : 2 * main + rest]], axis=1)
    second = jnp.concatenate([block[:, main : 2 * main], block[:, 2 * main + rest :]], axis=1)
    return first, second


def join_pair(first, second):
    main, rest = parts_of(first.shape[1] * 4)
    return jnp.concatenate(
        [first[:, :main], second[:, :main], first[:, main:], second[:, main:]], axis=1
    )


def ordered(own, other, first):
    return jnp.where(first, jnp.stack([own, other]), jnp.stack([other, own]))


def halves(row):
    high = row.astype(BF16)
    return high, (row - high.astype(F32)).astype(BF16)


def with_rows(block, *rows):
    shape = (EXTRA, block.shape[1])
    which = lax.broadcasted_iota(jnp.int32, shape, 0)
    tail = jnp.zeros(shape, BF16)
    for k, half in enumerate([half for row in rows for half in halves(row)]):
        tail = jnp.where(which == k, half[None, :], tail)
    return jnp.concatenate([block.astype(BF16), tail], axis=0)


def row_of(packed_rows, k=0):
    at_row = packed_rows.shape[0] - EXTRA + 2 * k
    return packed_rows[at_row].astype(F32) + packed_rows[at_row + 1].astype(F32)


def block_of(packed_rows):
    return packed_rows[: packed_rows.shape[0] - EXTRA].astype(F32)


def derivatives(gate, up, back):
    hidden, pull = jax.vjp(lambda g, u: jax.nn.gelu(g, approximate=True) * u, gate, up)
    return pull(back)


def shards(tokens, hidden_grad, norm_gain, w_gate, w_up):
    rows, width = w_gate.shape
    group = tokens.shape[0]
    features = norm_gain.shape[0]
    own_rows = features // 16
    barrier = lax.optimization_barrier

    zh, x, core, tp, sec = (unsigned(lax.axis_index(a)) for a in (*DP, *COLS))
    steps = (1, 3, 2)
    far_zh, other_core = 1 - zh, 1 - core
    first_core = core == 0
    x_to = {by: (x + by) & 3 for by in range(4)}
    sec_to = {by: (sec + by) & 3 for by in range(4)}
    tp_to = {by: (tp + by) & 3 for by in range(4)}
    offset = (tp * 4 + sec) * own_rows
    tp_to, offset, hidden_grad = barrier((tp_to, offset, hidden_grad))

    own_t = tokens.T
    far_t = swapped(own_t, "zh")

    near_own, near_other = packed(0, w_gate, w_up, hidden_grad)
    hidden_grad, near_own = barrier((hidden_grad, near_own))
    away_own, away_other, backs = packed(1, w_gate, w_up, hidden_grad)
    near_other = swapped(near_other, "core")
    away_other, far_t = barrier((away_other, far_t))
    away_own, away_other = swapped(away_own, "zh"), swapped(away_other, "zh")

    near = ordered(near_own[:rows], near_other[:rows], first_core)
    near, own_t = barrier((near, own_t))
    near_got = [turned(near, "x", by) for by in steps]

    both = jnp.concatenate([own_t, far_t], axis=1)
    both, near_got[0], near_got[1] = barrier((both, near_got[0], near_got[1]))
    section_got = [turned(both, "sec", by) for by in steps]

    near_got[0], near_got[1], backs, late_first = barrier(
        (near_got[0], near_got[1], backs, first_core)
    )
    away_other = swapped(away_other, "core")
    backs = swapped(backs, "zh")
    away = ordered(away_own, away_other, late_first)
    late = {}
    away, late[0], late[1], late[2], late[3] = barrier((away, *(sec_to[by] for by in range(4))))
    away_got = [turned(away, "x", by) for by in steps]

    inputs = jnp.zeros((4, *both.shape), BF16)
    for by, piece in zip((0, 3, 1, 2), (both, *section_got)):
        inputs = put(inputs, piece, late[by])
    inputs = inputs.reshape(features, 2 * group)
    wide = inputs.astype(F32)
    inv_rms = lax.rsqrt(jnp.mean(wide * wide, axis=0) + EPS)
    normed = (wide * inv_rms * norm_gain[:, None]).astype(BF16)
    normed, away_got[0] = barrier((normed, away_got[0]))
    normed_other, away_got[2] = barrier((swapped(normed, "core"), away_got[2]))
    normed = jnp.concatenate([normed, normed_other], axis=1)

    backs, *away_got = barrier((backs, *away_got))
    full = jnp.zeros((2, 4, 2, rows, width // 2), BF16)
    for pieces, place in (((near, *near_got), zh), ((away, *away_got), far_zh)):
        for by, piece in zip((0, 3, 1, 2), pieces):
            full = put(full, piece, place, x_to[by])
    full = full.reshape(features, -1)
    back = jnp.concatenate(
        [
            half
            for block in (near_own[rows:], backs[0], near_other[rows:], swapped(backs[1], "core"))
            for half in split_pair(block)
        ],
        axis=0,
    )

    product = lax.dot_general(
        normed, full, (((0,), (0,)), ((), ())), preferred_element_type=F32
    )
    gate, up = split_pair(product)
    d_gate, d_up = derivatives(gate, up, back.astype(F32))
    d_gate, d_up = d_gate.astype(BF16), d_up.astype(BF16)
    row_part = jnp.sum(d_gate.astype(F32) * gate + d_up.astype(F32) * up, axis=1)
    d_both = join_pair(d_gate, d_up)

    def d_normed(d):
        return lax.dot_general(full, d, (((1,), (1,)), ((), ())), preferred_element_type=F32)

    by_rows = normed.reshape(2, 4, 2 * rows, 4 * group)

    def part(zplace, xplace):
        return jnp.dot(as_block(by_rows, zplace, xplace), d_both, preferred_element_type=F32)

    away_parts = [part(far_zh, x_to[by]).astype(BF16) for by in steps]
    away_got = [turned(p, "x", by) for p, by in zip(away_parts, steps)]

    got = swapped(d_normed(d_both[2 * group :]).astype(BF16), "core")
    got, late_zh = barrier((got, zh))
    near_parts = [part(late_zh, x_to[by]).astype(BF16) for by in steps]
    row = row_part[: 2 * group] + swapped(row_part[2 * group :], "core")
    mine = d_normed(d_both[: 2 * group]) + got.astype(F32)
    mine = mine.reshape(4, 4, own_rows, 2 * group)

    def section(index):
        zero = jnp.uint32(0)
        block = lax.dynamic_slice(
            mine, (zero, index, zero, zero), (4, 1, own_rows, 2 * group)
        )
        return block.reshape(4 * own_rows, 2 * group)

    sends = [with_rows(section(sec_to[by]), row) for by in steps]
    g_away = (part(far_zh, x) + sum(g.astype(F32) for g in away_got)).astype(BF16)
    g_away, *rest = barrier((g_away, *sends, *near_parts))
    sends, near_parts = rest[:3], rest[3:]
    got = [turned(s, "sec", by) for s, by in zip(sends, steps)]
    near_got = [turned(p, "x", by) for p, by in zip(near_parts, steps)]
    g_away = g_away.reshape(2, rows, -1)
    away_keep = swapped(as_block(g_away, core), "zh")
    away_give = swapped(as_block(g_away, other_core), "zh")
    late = {}
    away_give, late[1], late[3], late[2] = barrier((away_give, *(tp_to[by] for by in steps)))

    total = section(sec) + sum(block_of(g) for g in got)
    row = row + sum(row_of(g) for g in got)
    mine = total.reshape(4, own_rows, 2 * group)
    sends = [with_rows(as_block(mine, late[by]), row) for by in steps]
    got = [turned(s, "tp", by) for s, by in zip(sends, steps)]
    total = as_block(mine, tp) + sum(block_of(g) for g in got)
    row = row + sum(row_of(g) for g in got)

    own_inputs = lax.dynamic_slice(inputs, (offset, jnp.uint32(0)), (own_rows, 2 * group))
    own_inputs = own_inputs.astype(F32)
    own_gain = lax.dynamic_slice(norm_gain, (offset,), (own_rows,))[:, None]
    gain_part = jnp.sum(total * own_inputs * inv_rms, axis=1)
    gain_rows = jnp.pad(gain_part, (0, 2 * group - own_rows)).reshape(2, group)
    send = with_rows(total[:, group:], row[group:], gain_rows[0], gain_rows[1])
    send, near_got[0], late_zh = barrier((send, near_got[0], zh))
    got = swapped(send, "zh")
    g_near = part(late_zh, x) + sum(g.astype(F32) for g in near_got)
    g_near = g_near.astype(BF16).reshape(2, rows, -1)
    give = swapped(jnp.stack([as_block(g_near, other_core), away_give]), "core")
    grad_gain = gain_part + jnp.concatenate([row_of(got, 1), row_of(got, 2)])[:own_rows]
    grad_gain = grad_gain + swapped(grad_gain, "core")
    grad_gain = grad_gain + sum(turned(grad_gain, "x", by) for by in steps)
    d_own, row_sum = total[:, :group] + block_of(got), row[:group] + row_of(got)
    inv = inv_rms[:group]
    own_inputs = own_inputs[:, :group]
    grad_tokens = inv * own_gain * d_own - own_inputs * (inv**2 * row_sum / features)
    grad_gate, grad_up = joined(g_near, away_keep, give)
    return grad_tokens.T.astype(BF16), grad_gain, grad_gate, grad_up


def solution(mesh):
    split = Mesh(
        mesh.devices.reshape(2, 4, 2, mesh.shape["tp"], mesh.shape["section"]),
        (*DP, *COLS),
    )
    weights = P(DP, COLS)
    return jax.shard_map(
        shards,
        mesh=split,
        in_specs=(P(DP, "sec"), weights, P(), weights, weights),
        out_specs=(weights, P(COLS), weights, weights),
        check_vma=False,
    )
```

```python
import functools

import jax
import jax.numpy as jnp
from jax import lax
from jax.experimental import pallas as pl
from jax.experimental.pallas import tpu as pltpu
from jax.sharding import Mesh
from jax.sharding import PartitionSpec as P

DP = ("zh", "x", "core")
COLS = ("tp", "sec")
EPS = 1e-06
LANES = 128
EXTRA = 16
F32 = jnp.float32
BF16 = jnp.bfloat16
SDS = jax.ShapeDtypeStruct


def turned(array, axis, by):
    n = lax.axis_size(axis)
    return lax.ppermute(array, axis, [(i, (i + by) % n) for i in range(n)])


def swapped(array, axis):
    return turned(array, axis, 1)


def unsigned(index):
    return index.astype(jnp.uint32)


def as_block(array, *lead):
    n = len(lead)
    zeros = [jnp.uint32(0)] * (array.ndim - n)
    part = lax.dynamic_slice(array, (*lead, *zeros), (*([1] * n), *array.shape[n:]))
    return part.reshape(array.shape[n:])


def put(array, part, *lead):
    zeros = [jnp.uint32(0)] * (array.ndim - len(lead))
    part = part.reshape(*([1] * len(lead)), *array.shape[len(lead) :])
    return lax.dynamic_update_slice(array, part, (*lead, *zeros))


def parts_of(width):
    main = width // LANES // 4 * LANES
    rest = width // 4 - main
    return main, rest


def pack_kernel(main, rest, aways, gate_ref, up_ref, back_ref, *outs):
    half = back_ref.shape[0] // 2
    zh, core = lax.axis_index("zh"), lax.axis_index("core")
    rows = gate_ref.shape[0]
    if aways:
        weights, backs = outs[:2], [outs[2].at[0], outs[2].at[1]]
    else:
        weights = [out.at[pl.ds(0, rows)] for out in outs]
        backs = [out.at[pl.ds(rows, half)] for out in outs]
    sources = (
        (weights, gate_ref, up_ref),
        (backs, back_ref.at[pl.ds(0, half)], back_ref.at[pl.ds(half, half)]),
    )
    for other in range(2):
        q = (zh ^ aways) * 2 + (core ^ other)
        wide = pl.ds(pl.multiple_of(q * main, LANES), main)
        for targets, first, second in sources:
            out = targets[other]
            out[:, pl.ds(0, main)] = first[:, wide]
            out[:, pl.ds(main, main)] = second[:, wide]
            thin = []
            for ref in (first, second):
                tail = ref[:, pl.ds(4 * main, 4 * rest)]
                turn = pltpu.roll(tail.astype(F32), ((4 - q) & 3) * rest, 1)
                thin.append(turn[:, :rest].astype(BF16))
            out[:, pl.ds(2 * main, 2 * rest)] = jnp.concatenate(thin, axis=1)


def packed(aways, w_gate, w_up, hidden_grad):
    rows, width = w_gate.shape
    main, rest = parts_of(width)
    half = hidden_grad.shape[0] // 2
    if aways:
        outs = [(rows, width // 2), (rows, width // 2), (2, half, width // 2)]
    else:
        outs = [(rows + half, width // 2)] * 2
    return pl.pallas_call(
        functools.partial(pack_kernel, main, rest, aways),
        out_shape=[pltpu.VMEM(shape, BF16) for shape in outs],
        in_specs=[pl.BlockSpec(memory_space=pltpu.VMEM)] * 3,
        out_specs=[pl.BlockSpec(memory_space=pltpu.VMEM)] * len(outs),
        name="pack",
    )(w_gate, w_up, hidden_grad)


def join_kernel(main, rest, near_ref, keep_ref, give_ref, gate_ref, up_ref):
    zh, core = lax.axis_index("zh"), lax.axis_index("core")
    tails = [[None] * 4, [None] * 4]
    for aways in range(2):
        for other in range(2):
            ref = give_ref.at[aways] if other else keep_ref if aways else near_ref.at[core]
            q = (zh ^ aways) * 2 + (core ^ other)
            wide = pl.ds(pl.multiple_of(q * main, LANES), main)
            gate_ref[:, wide] = ref[:, pl.ds(0, main)]
            up_ref[:, wide] = ref[:, pl.ds(main, main)]
            tail = ref[:, pl.ds(2 * main, 2 * rest)]
            for i in range(2):
                thin = tail[:, i * rest : (i + 1) * rest]
                for k in range(4):
                    old = tails[i][k]
                    tails[i][k] = thin if old is None else jnp.where(q == k, thin, old)
    gate_ref[:, pl.ds(4 * main, 4 * rest)] = jnp.concatenate(tails[0], axis=1)
    up_ref[:, pl.ds(4 * main, 4 * rest)] = jnp.concatenate(tails[1], axis=1)


def joined(near, keep, give):
    rows, half = keep.shape
    main, rest = parts_of(half * 2)
    out = SDS((rows, half * 2), BF16)
    return pl.pallas_call(
        functools.partial(join_kernel, main, rest),
        out_shape=(out, out),
        in_specs=[pl.BlockSpec(memory_space=pltpu.VMEM)] * 3,
        out_specs=(pl.BlockSpec(memory_space=pltpu.VMEM),) * 2,
        name="join",
    )(near, keep, give)


def split_pair(block):
    main, rest = parts_of(block.shape[1] * 2)
    first = jnp.concatenate([block[:, :main], block[:, 2 * main : 2 * main + rest]], axis=1)
    second = jnp.concatenate([block[:, main : 2 * main], block[:, 2 * main + rest :]], axis=1)
    return first, second


def join_pair(first, second):
    main, rest = parts_of(first.shape[1] * 4)
    return jnp.concatenate(
        [first[:, :main], second[:, :main], first[:, main:], second[:, main:]], axis=1
    )


def ordered(own, other, first):
    return jnp.where(first, jnp.stack([own, other]), jnp.stack([other, own]))


def halves(row):
    high = row.astype(BF16)
    return high, (row - high.astype(F32)).astype(BF16)


def with_rows(block, *rows):
    shape = (EXTRA, block.shape[1])
    which = lax.broadcasted_iota(jnp.int32, shape, 0)
    tail = jnp.zeros(shape, BF16)
    for k, half in enumerate([half for row in rows for half in halves(row)]):
        tail = jnp.where(which == k, half[None, :], tail)
    return jnp.concatenate([block.astype(BF16), tail], axis=0)


def row_of(packed_rows, k=0):
    at_row = packed_rows.shape[0] - EXTRA + 2 * k
    return packed_rows[at_row].astype(F32) + packed_rows[at_row + 1].astype(F32)


def block_of(packed_rows):
    return packed_rows[: packed_rows.shape[0] - EXTRA].astype(F32)


def derivatives(gate, up, back):
    hidden, pull = jax.vjp(lambda g, u: jax.nn.gelu(g, approximate=True) * u, gate, up)
    return pull(back)


def shards(tokens, hidden_grad, norm_gain, w_gate, w_up):
    rows, width = w_gate.shape
    group = tokens.shape[0]
    features = norm_gain.shape[0]
    own_rows = features // 16
    barrier = lax.optimization_barrier

    zh, x, core, tp, sec = (unsigned(lax.axis_index(a)) for a in (*DP, *COLS))
    steps = (1, 3, 2)
    far_zh, other_core = 1 - zh, 1 - core
    first_core = core == 0
    x_to = {by: (x + by) & 3 for by in range(4)}
    sec_to = {by: (sec + by) & 3 for by in range(4)}
    tp_to = {by: (tp + by) & 3 for by in range(4)}
    offset = (tp * 4 + sec) * own_rows
    tp_to, offset, hidden_grad = barrier((tp_to, offset, hidden_grad))

    own_t = tokens.T
    far_t = swapped(own_t, "zh")

    near_own, near_other = packed(0, w_gate, w_up, hidden_grad)
    hidden_grad, near_own = barrier((hidden_grad, near_own))
    away_own, away_other, backs = packed(1, w_gate, w_up, hidden_grad)
    near_other = swapped(near_other, "core")
    away_other, far_t = barrier((away_other, far_t))
    away_own, away_other = swapped(away_own, "zh"), swapped(away_other, "zh")

    near = ordered(near_own[:rows], near_other[:rows], first_core)
    near, own_t = barrier((near, own_t))
    near_got = [turned(near, "x", by) for by in steps]

    both = jnp.concatenate([own_t, far_t], axis=1)
    both, near_got[0], near_got[1] = barrier((both, near_got[0], near_got[1]))
    section_got = [turned(both, "sec", by) for by in steps]

    near_got[0], near_got[1], backs, late_first = barrier(
        (near_got[0], near_got[1], backs, first_core)
    )
    away_other = swapped(away_other, "core")
    backs = swapped(backs, "zh")
    away = ordered(away_own, away_other, late_first)
    late = {}
    away, late[0], late[1], late[2], late[3] = barrier((away, *(sec_to[by] for by in range(4))))
    away_got = [turned(away, "x", by) for by in steps]

    inputs = jnp.zeros((4, *both.shape), BF16)
    for by, piece in zip((0, 3, 1, 2), (both, *section_got)):
        inputs = put(inputs, piece, late[by])
    inputs = inputs.reshape(features, 2 * group)
    wide = inputs.astype(F32)
    inv_rms = lax.rsqrt(jnp.mean(wide * wide, axis=0) + EPS)
    normed = (wide * inv_rms * norm_gain[:, None]).astype(BF16)
    normed, away_got[0] = barrier((normed, away_got[0]))
    normed_other, away_got[2] = barrier((swapped(normed, "core"), away_got[2]))
    normed = jnp.concatenate([normed, normed_other], axis=1)

    backs, *away_got = barrier((backs, *away_got))
    full = jnp.zeros((2, 4, 2, rows, width // 2), BF16)
    for pieces, place in (((near, *near_got), zh), ((away, *away_got), far_zh)):
        for by, piece in zip((0, 3, 1, 2), pieces):
            full = put(full, piece, place, x_to[by])
    full = full.reshape(features, -1)
    back = jnp.concatenate(
        [
            half
            for block in (near_own[rows:], backs[0], near_other[rows:], swapped(backs[1], "core"))
            for half in split_pair(block)
        ],
        axis=0,
    )

    product = lax.dot_general(
        normed, full, (((0,), (0,)), ((), ())), preferred_element_type=F32
    )
    gate, up = split_pair(product)
    d_gate, d_up = derivatives(gate, up, back.astype(F32))
    d_gate, d_up = d_gate.astype(BF16), d_up.astype(BF16)
    row_part = jnp.sum(d_gate.astype(F32) * gate + d_up.astype(F32) * up, axis=1)
    d_both = join_pair(d_gate, d_up)

    def d_normed(d):
        return lax.dot_general(full, d, (((1,), (1,)), ((), ())), preferred_element_type=F32)

    by_rows = normed.reshape(2, 4, 2 * rows, 4 * group)

    def part(zplace, xplace):
        return jnp.dot(as_block(by_rows, zplace, xplace), d_both, preferred_element_type=F32)

    away_parts = [part(far_zh, x_to[by]).astype(BF16) for by in steps]
    near_parts = [part(zh, x_to[by]).astype(BF16) for by in steps]
    away_got = [turned(away_parts[k], "x", steps[k]) for k in (0, 1)]

    got = swapped(d_normed(d_both[2 * group :]).astype(BF16), "core")
    row = row_part[: 2 * group] + swapped(row_part[2 * group :], "core")
    mine = d_normed(d_both[: 2 * group]) + got.astype(F32)
    mine = mine.reshape(4, 4, own_rows, 2 * group)

    def section(index):
        zero = jnp.uint32(0)
        block = lax.dynamic_slice(
            mine, (zero, index, zero, zero), (4, 1, own_rows, 2 * group)
        )
        return block.reshape(4 * own_rows, 2 * group)

    sends = [with_rows(section(sec_to[by]), row) for by in steps]
    *away_got, away_parts[2], sends[0], sends[1], sends[2] = barrier(
        (*away_got, away_parts[2], *sends)
    )
    away_got.append(turned(away_parts[2], "x", 2))
    got = [turned(s, "sec", by) for s, by in zip(sends, steps)]
    away_got[2], *near_parts = barrier((away_got[2], *near_parts))
    near_got = [turned(p, "x", by) for p, by in zip(near_parts, steps)]
    g_away = part(far_zh, x) + sum(g.astype(F32) for g in away_got)
    g_away = g_away.astype(BF16).reshape(2, rows, -1)
    late = {}
    g_away, late[1], late[3], late[2] = barrier((g_away, *(tp_to[by] for by in steps)))
    away_keep = swapped(as_block(g_away, core), "zh")
    away_give = swapped(as_block(g_away, other_core), "zh")

    total = section(sec) + sum(block_of(g) for g in got)
    row = row + sum(row_of(g) for g in got)
    mine = total.reshape(4, own_rows, 2 * group)
    sends = [with_rows(as_block(mine, late[by]), row) for by in steps]
    got = [turned(s, "tp", by) for s, by in zip(sends, steps)]
    total = as_block(mine, tp) + sum(block_of(g) for g in got)
    row = row + sum(row_of(g) for g in got)

    own_inputs = lax.dynamic_slice(inputs, (offset, jnp.uint32(0)), (own_rows, 2 * group))
    own_inputs = own_inputs.astype(F32)
    own_gain = lax.dynamic_slice(norm_gain, (offset,), (own_rows,))[:, None]
    gain_part = jnp.sum(total * own_inputs * inv_rms, axis=1)
    gain_rows = jnp.pad(gain_part, (0, 2 * group - own_rows)).reshape(2, group)
    send = with_rows(total[:, group:], row[group:], gain_rows[0], gain_rows[1])
    send, near_got[0], near_got[1], late_zh = barrier((send, near_got[0], near_got[1], zh))
    got = swapped(send, "zh")
    g_near = part(late_zh, x) + sum(g.astype(F32) for g in near_got)
    g_near = g_near.astype(BF16).reshape(2, rows, -1)
    give = swapped(jnp.stack([as_block(g_near, other_core), away_give]), "core")
    grad_gain = gain_part + jnp.concatenate([row_of(got, 1), row_of(got, 2)])[:own_rows]
    grad_gain = grad_gain + swapped(grad_gain, "core")
    grad_gain = grad_gain + sum(turned(grad_gain, "x", by) for by in steps)
    d_own, row_sum = total[:, :group] + block_of(got), row[:group] + row_of(got)
    inv = inv_rms[:group]
    own_inputs = own_inputs[:, :group]
    grad_tokens = inv * own_gain * d_own - own_inputs * (inv**2 * row_sum / features)
    grad_gate, grad_up = joined(g_near, away_keep, give)
    return grad_tokens.T.astype(BF16), grad_gain, grad_gate, grad_up


def solution(mesh):
    split = Mesh(
        mesh.devices.reshape(2, 4, 2, mesh.shape["tp"], mesh.shape["section"]),
        (*DP, *COLS),
    )
    weights = P(DP, COLS)
    return jax.shard_map(
        shards,
        mesh=split,
        in_specs=(P(DP, "sec"), weights, P(), weights, weights),
        out_specs=(weights, P(COLS), weights, weights),
        check_vma=False,
    )
```

```python
import functools

import jax
import jax.numpy as jnp
from jax import lax
from jax.experimental import pallas as pl
from jax.experimental.pallas import tpu as pltpu
from jax.sharding import Mesh
from jax.sharding import PartitionSpec as P

DP = ("zh", "x", "core")
COLS = ("tp", "sec")
EPS = 1e-06
LANES = 128
EXTRA = 16
F32 = jnp.float32
BF16 = jnp.bfloat16
SDS = jax.ShapeDtypeStruct


def turned(array, axis, by):
    n = lax.axis_size(axis)
    return lax.ppermute(array, axis, [(i, (i + by) % n) for i in range(n)])


def swapped(array, axis):
    return turned(array, axis, 1)


def crossed(array):
    return lax.ppermute(array, ("zh", "core"), [(i, 3 - i) for i in range(4)])


def unsigned(index):
    return index.astype(jnp.uint32)


def as_block(array, *lead):
    n = len(lead)
    zeros = [jnp.uint32(0)] * (array.ndim - n)
    part = lax.dynamic_slice(array, (*lead, *zeros), (*([1] * n), *array.shape[n:]))
    return part.reshape(array.shape[n:])


def put(array, part, *lead):
    zeros = [jnp.uint32(0)] * (array.ndim - len(lead))
    part = part.reshape(*([1] * len(lead)), *array.shape[len(lead) :])
    return lax.dynamic_update_slice(array, part, (*lead, *zeros))


def parts_of(width):
    main = width // LANES // 4 * LANES
    rest = width // 4 - main
    return main, rest


def pack_kernel(main, rest, aways, gate_ref, up_ref, back_ref, *outs):
    half = back_ref.shape[0] // 2
    zh, core = lax.axis_index("zh"), lax.axis_index("core")
    rows = gate_ref.shape[0]
    if aways:
        weights, backs = outs[:2], outs[2:]
    else:
        weights = [out.at[pl.ds(0, rows)] for out in outs]
        backs = [out.at[pl.ds(rows, half)] for out in outs]
    sources = (
        (weights, gate_ref, up_ref),
        (backs, back_ref.at[pl.ds(0, half)], back_ref.at[pl.ds(half, half)]),
    )
    for other in range(2):
        q = (zh ^ aways) * 2 + (core ^ other)
        wide = pl.ds(pl.multiple_of(q * main, LANES), main)
        for targets, first, second in sources:
            out = targets[other]
            out[:, pl.ds(0, main)] = first[:, wide]
            out[:, pl.ds(main, main)] = second[:, wide]
            thin = []
            for ref in (first, second):
                tail = ref[:, pl.ds(4 * main, 4 * rest)]
                turn = pltpu.roll(tail.astype(F32), ((4 - q) & 3) * rest, 1)
                thin.append(turn[:, :rest].astype(BF16))
            out[:, pl.ds(2 * main, 2 * rest)] = jnp.concatenate(thin, axis=1)


def packed(aways, w_gate, w_up, hidden_grad):
    rows, width = w_gate.shape
    main, rest = parts_of(width)
    half = hidden_grad.shape[0] // 2
    if aways:
        outs = [(rows, width // 2), (rows, width // 2), *[(half, width // 2)] * 2]
    else:
        outs = [(rows + half, width // 2)] * 2
    return pl.pallas_call(
        functools.partial(pack_kernel, main, rest, aways),
        out_shape=[pltpu.VMEM(shape, BF16) for shape in outs],
        in_specs=[pl.BlockSpec(memory_space=pltpu.VMEM)] * 3,
        out_specs=[pl.BlockSpec(memory_space=pltpu.VMEM)] * len(outs),
        name="pack",
    )(w_gate, w_up, hidden_grad)


def join_kernel(main, rest, near_ref, keep_ref, give_ref, gate_ref, up_ref):
    zh, core = lax.axis_index("zh"), lax.axis_index("core")
    tails = [[None] * 4, [None] * 4]
    for aways in range(2):
        for other in range(2):
            ref = give_ref.at[aways] if other else keep_ref if aways else near_ref.at[core]
            q = (zh ^ aways) * 2 + (core ^ other)
            wide = pl.ds(pl.multiple_of(q * main, LANES), main)
            gate_ref[:, wide] = ref[:, pl.ds(0, main)]
            up_ref[:, wide] = ref[:, pl.ds(main, main)]
            tail = ref[:, pl.ds(2 * main, 2 * rest)]
            for i in range(2):
                thin = tail[:, i * rest : (i + 1) * rest]
                for k in range(4):
                    old = tails[i][k]
                    tails[i][k] = thin if old is None else jnp.where(q == k, thin, old)
    gate_ref[:, pl.ds(4 * main, 4 * rest)] = jnp.concatenate(tails[0], axis=1)
    up_ref[:, pl.ds(4 * main, 4 * rest)] = jnp.concatenate(tails[1], axis=1)


def joined(near, keep, give):
    rows, half = keep.shape
    main, rest = parts_of(half * 2)
    out = SDS((rows, half * 2), BF16)
    return pl.pallas_call(
        functools.partial(join_kernel, main, rest),
        out_shape=(out, out),
        in_specs=[pl.BlockSpec(memory_space=pltpu.VMEM)] * 3,
        out_specs=(pl.BlockSpec(memory_space=pltpu.VMEM),) * 2,
        name="join",
    )(near, keep, give)


def split_pair(block):
    main, rest = parts_of(block.shape[1] * 2)
    first = jnp.concatenate([block[:, :main], block[:, 2 * main : 2 * main + rest]], axis=1)
    second = jnp.concatenate([block[:, main : 2 * main], block[:, 2 * main + rest :]], axis=1)
    return first, second


def join_pair(first, second):
    main, rest = parts_of(first.shape[1] * 4)
    return jnp.concatenate(
        [first[:, :main], second[:, :main], first[:, main:], second[:, main:]], axis=1
    )


def ordered(own, other, first):
    return jnp.where(first, jnp.stack([own, other]), jnp.stack([other, own]))


def halves(row):
    high = row.astype(BF16)
    return high, (row - high.astype(F32)).astype(BF16)


def with_rows(block, *rows):
    shape = (EXTRA, block.shape[1])
    which = lax.broadcasted_iota(jnp.int32, shape, 0)
    tail = jnp.zeros(shape, BF16)
    for k, half in enumerate([half for row in rows for half in halves(row)]):
        tail = jnp.where(which == k, half[None, :], tail)
    return jnp.concatenate([block.astype(BF16), tail], axis=0)


def row_of(packed_rows, k=0):
    at_row = packed_rows.shape[0] - EXTRA + 2 * k
    return packed_rows[at_row].astype(F32) + packed_rows[at_row + 1].astype(F32)


def block_of(packed_rows):
    return packed_rows[: packed_rows.shape[0] - EXTRA].astype(F32)


def derivatives(gate, up, back):
    hidden, pull = jax.vjp(lambda g, u: jax.nn.gelu(g, approximate=True) * u, gate, up)
    return pull(back)


def shards(tokens, hidden_grad, norm_gain, w_gate, w_up):
    rows, width = w_gate.shape
    group = tokens.shape[0]
    features = norm_gain.shape[0]
    own_rows = features // 16
    barrier = lax.optimization_barrier

    zh, x, core, tp, sec = (unsigned(lax.axis_index(a)) for a in (*DP, *COLS))
    steps = (1, 3, 2)
    far_zh, other_core = 1 - zh, 1 - core
    first_core = core == 0
    x_to = {by: (x + by) & 3 for by in range(4)}
    sec_to = {by: (sec + by) & 3 for by in range(4)}
    tp_to = {by: (tp + by) & 3 for by in range(4)}
    offset = (tp * 4 + sec) * own_rows
    tp_to, offset, hidden_grad = barrier((tp_to, offset, hidden_grad))

    own_t = tokens.T
    far_t = swapped(own_t, "zh")

    near_own, near_other = packed(0, w_gate, w_up, hidden_grad)
    hidden_grad, near_own = barrier((hidden_grad, near_own))
    away_own, away_other, back_same, back_cross = packed(1, w_gate, w_up, hidden_grad)
    near_other = swapped(near_other, "core")
    away_other, far_t = barrier((away_other, far_t))
    away_own, away_other = swapped(away_own, "zh"), swapped(away_other, "zh")

    near = ordered(near_own[:rows], near_other[:rows], first_core)
    near, own_t = barrier((near, own_t))
    near_got = [turned(near, "x", by) for by in steps]

    both = jnp.concatenate([own_t, far_t], axis=1)
    both, near_got[0], near_got[1] = barrier((both, near_got[0], near_got[1]))
    section_got = [turned(both, "sec", by) for by in steps]

    near_got[0], near_got[1], back_same, back_cross, late_first = barrier(
        (near_got[0], near_got[1], back_same, back_cross, first_core)
    )
    away_other = swapped(away_other, "core")
    back_same, back_cross = swapped(back_same, "zh"), crossed(back_cross)
    away = ordered(away_own, away_other, late_first)
    late = {}
    away, late[0], late[1], late[2], late[3] = barrier((away, *(sec_to[by] for by in range(4))))
    away_got = [turned(away, "x", by) for by in steps]

    inputs = jnp.zeros((4, *both.shape), BF16)
    for by, piece in zip((0, 3, 1, 2), (both, *section_got)):
        inputs = put(inputs, piece, late[by])
    inputs = inputs.reshape(features, 2 * group)
    wide = inputs.astype(F32)
    inv_rms = lax.rsqrt(jnp.mean(wide * wide, axis=0) + EPS)
    normed = (wide * inv_rms * norm_gain[:, None]).astype(BF16)
    normed, away_got[0] = barrier((normed, away_got[0]))
    normed_other, away_got[2] = barrier((swapped(normed, "core"), away_got[2]))
    normed = jnp.concatenate([normed, normed_other], axis=1)

    back_same, back_cross, *away_got = barrier((back_same, back_cross, *away_got))
    full = jnp.zeros((2, 4, 2, rows, width // 2), BF16)
    for pieces, place in (((near, *near_got), zh), ((away, *away_got), far_zh)):
        for by, piece in zip((0, 3, 1, 2), pieces):
            full = put(full, piece, place, x_to[by])
    full = full.reshape(features, -1)
    back = jnp.concatenate(
        [
            half
            for block in (near_own[rows:], back_same, near_other[rows:], back_cross)
            for half in split_pair(block)
        ],
        axis=0,
    )

    product = lax.dot_general(
        normed, full, (((0,), (0,)), ((), ())), preferred_element_type=F32
    )
    gate, up = split_pair(product)
    d_gate, d_up = derivatives(gate, up, back.astype(F32))
    d_gate, d_up = d_gate.astype(BF16), d_up.astype(BF16)
    row_part = jnp.sum(d_gate.astype(F32) * gate + d_up.astype(F32) * up, axis=1)
    d_both = join_pair(d_gate, d_up)

    def d_normed(d):
        return lax.dot_general(full, d, (((1,), (1,)), ((), ())), preferred_element_type=F32)

    by_rows = normed.reshape(2, 4, 2 * rows, 4 * group)

    def part(zplace, xplace):
        return jnp.dot(as_block(by_rows, zplace, xplace), d_both, preferred_element_type=F32)

    away_parts = [part(far_zh, x_to[by]).astype(BF16) for by in steps]
    near_parts = [part(zh, x_to[by]).astype(BF16) for by in steps]
    away_got = [turned(away_parts[k], "x", steps[k]) for k in (0, 1)]

    got = swapped(d_normed(d_both[2 * group :]).astype(BF16), "core")
    row = row_part[: 2 * group] + swapped(row_part[2 * group :], "core")
    mine = d_normed(d_both[: 2 * group]) + got.astype(F32)
    mine = mine.reshape(4, 4, own_rows, 2 * group)

    def section(index):
        zero = jnp.uint32(0)
        block = lax.dynamic_slice(
            mine, (zero, index, zero, zero), (4, 1, own_rows, 2 * group)
        )
        return block.reshape(4 * own_rows, 2 * group)

    sends = [with_rows(section(sec_to[by]), row) for by in steps]
    *away_got, away_parts[2], sends[0], sends[1], sends[2] = barrier(
        (*away_got, away_parts[2], *sends)
    )
    away_got.append(turned(away_parts[2], "x", 2))
    got = [turned(s, "sec", by) for s, by in zip(sends, steps)]
    away_got[2], *near_parts = barrier((away_got[2], *near_parts))
    near_got = [turned(p, "x", by) for p, by in zip(near_parts, steps)]
    g_away = part(far_zh, x) + sum(g.astype(F32) for g in away_got)
    g_away = g_away.astype(BF16).reshape(2, rows, -1)
    late = {}
    g_away, late[1], late[3], late[2] = barrier((g_away, *(tp_to[by] for by in steps)))
    away_keep = swapped(as_block(g_away, core), "zh")
    away_give = swapped(as_block(g_away, other_core), "zh")

    total = section(sec) + sum(block_of(g) for g in got)
    row = row + sum(row_of(g) for g in got)
    mine = total.reshape(4, own_rows, 2 * group)
    sends = [with_rows(as_block(mine, late[by]), row) for by in steps]
    got = [turned(s, "tp", by) for s, by in zip(sends, steps)]
    total = as_block(mine, tp) + sum(block_of(g) for g in got)
    row = row + sum(row_of(g) for g in got)

    own_inputs = lax.dynamic_slice(inputs, (offset, jnp.uint32(0)), (own_rows, 2 * group))
    own_inputs = own_inputs.astype(F32)
    own_gain = lax.dynamic_slice(norm_gain, (offset,), (own_rows,))[:, None]
    gain_part = jnp.sum(total * own_inputs * inv_rms, axis=1)
    gain_rows = jnp.pad(gain_part, (0, 2 * group - own_rows)).reshape(2, group)
    send = with_rows(total[:, group:], row[group:], gain_rows[0], gain_rows[1])
    send, near_got[0], near_got[1], late_zh = barrier((send, near_got[0], near_got[1], zh))
    got = swapped(send, "zh")
    g_near = part(late_zh, x) + sum(g.astype(F32) for g in near_got)
    g_near = g_near.astype(BF16).reshape(2, rows, -1)
    grad_gain = gain_part + jnp.concatenate([row_of(got, 1), row_of(got, 2)])[:own_rows]
    grad_gain = grad_gain + swapped(grad_gain, "core")
    late_core, grad_gain = barrier((other_core, grad_gain))
    give = swapped(jnp.stack([as_block(g_near, late_core), away_give]), "core")
    grad_gain = grad_gain + sum(turned(grad_gain, "x", by) for by in steps)
    d_own, row_sum = total[:, :group] + block_of(got), row[:group] + row_of(got)
    inv = inv_rms[:group]
    own_inputs = own_inputs[:, :group]
    grad_tokens = inv * own_gain * d_own - own_inputs * (inv**2 * row_sum / features)
    grad_gate, grad_up = joined(g_near, away_keep, give)
    return grad_tokens.T.astype(BF16), grad_gain, grad_gate, grad_up


def solution(mesh):
    split = Mesh(
        mesh.devices.reshape(2, 4, 2, mesh.shape["tp"], mesh.shape["section"]),
        (*DP, *COLS),
    )
    weights = P(DP, COLS)
    return jax.shard_map(
        shards,
        mesh=split,
        in_specs=(P(DP, "sec"), weights, P(), weights, weights),
        out_specs=(weights, P(COLS), weights, weights),
        check_vma=False,
    )
```

```python
import functools

import jax
import jax.numpy as jnp
from jax import lax
from jax.experimental import pallas as pl
from jax.experimental.pallas import tpu as pltpu
from jax.sharding import Mesh
from jax.sharding import PartitionSpec as P

DP = ("zh", "x", "core")
COLS = ("tp", "sec")
EPS = 1e-06
LANES = 128
EXTRA = 16
F32 = jnp.float32
BF16 = jnp.bfloat16
SDS = jax.ShapeDtypeStruct


def turned(array, axis, by):
    n = lax.axis_size(axis)
    return lax.ppermute(array, axis, [(i, (i + by) % n) for i in range(n)])


def swapped(array, axis):
    return turned(array, axis, 1)


def unsigned(index):
    return index.astype(jnp.uint32)


def as_block(array, *lead):
    n = len(lead)
    zeros = [jnp.uint32(0)] * (array.ndim - n)
    part = lax.dynamic_slice(array, (*lead, *zeros), (*([1] * n), *array.shape[n:]))
    return part.reshape(array.shape[n:])


def put(array, part, *lead):
    zeros = [jnp.uint32(0)] * (array.ndim - len(lead))
    part = part.reshape(*([1] * len(lead)), *array.shape[len(lead) :])
    return lax.dynamic_update_slice(array, part, (*lead, *zeros))


def parts_of(width):
    main = width // LANES // 4 * LANES
    rest = width // 4 - main
    return main, rest


def pack_kernel(main, rest, aways, gate_ref, up_ref, back_ref, *outs):
    half = back_ref.shape[0] // 2
    zh, core = lax.axis_index("zh"), lax.axis_index("core")
    rows = gate_ref.shape[0]
    if aways:
        weights, backs = outs[:2], [outs[2].at[0], outs[2].at[1]]
    else:
        weights = [out.at[pl.ds(0, rows)] for out in outs]
        backs = [out.at[pl.ds(rows, half)] for out in outs]
    sources = (
        (weights, gate_ref, up_ref),
        (backs, back_ref.at[pl.ds(0, half)], back_ref.at[pl.ds(half, half)]),
    )
    for other in range(2):
        q = (zh ^ aways) * 2 + (core ^ other)
        wide = pl.ds(pl.multiple_of(q * main, LANES), main)
        for targets, first, second in sources:
            out = targets[other]
            out[:, pl.ds(0, main)] = first[:, wide]
            out[:, pl.ds(main, main)] = second[:, wide]
            thin = []
            for ref in (first, second):
                tail = ref[:, pl.ds(4 * main, 4 * rest)]
                turn = pltpu.roll(tail.astype(F32), ((4 - q) & 3) * rest, 1)
                thin.append(turn[:, :rest].astype(BF16))
            out[:, pl.ds(2 * main, 2 * rest)] = jnp.concatenate(thin, axis=1)


def packed(aways, w_gate, w_up, hidden_grad):
    rows, width = w_gate.shape
    main, rest = parts_of(width)
    half = hidden_grad.shape[0] // 2
    if aways:
        outs = [(rows, width // 2), (rows, width // 2), (2, half, width // 2)]
    else:
        outs = [(rows + half, width // 2)] * 2
    return pl.pallas_call(
        functools.partial(pack_kernel, main, rest, aways),
        out_shape=[pltpu.VMEM(shape, BF16) for shape in outs],
        in_specs=[pl.BlockSpec(memory_space=pltpu.VMEM)] * 3,
        out_specs=[pl.BlockSpec(memory_space=pltpu.VMEM)] * len(outs),
        name="pack",
    )(w_gate, w_up, hidden_grad)


def join_kernel(main, rest, near_ref, keep_ref, give_ref, gate_ref, up_ref):
    zh, core = lax.axis_index("zh"), lax.axis_index("core")
    tails = [[None] * 4, [None] * 4]
    for aways in range(2):
        for other in range(2):
            ref = give_ref.at[aways] if other else keep_ref if aways else near_ref.at[core]
            q = (zh ^ aways) * 2 + (core ^ other)
            wide = pl.ds(pl.multiple_of(q * main, LANES), main)
            gate_ref[:, wide] = ref[:, pl.ds(0, main)]
            up_ref[:, wide] = ref[:, pl.ds(main, main)]
            tail = ref[:, pl.ds(2 * main, 2 * rest)]
            for i in range(2):
                thin = tail[:, i * rest : (i + 1) * rest]
                for k in range(4):
                    old = tails[i][k]
                    tails[i][k] = thin if old is None else jnp.where(q == k, thin, old)
    gate_ref[:, pl.ds(4 * main, 4 * rest)] = jnp.concatenate(tails[0], axis=1)
    up_ref[:, pl.ds(4 * main, 4 * rest)] = jnp.concatenate(tails[1], axis=1)


def joined(near, keep, give):
    rows, half = keep.shape
    main, rest = parts_of(half * 2)
    out = SDS((rows, half * 2), BF16)
    return pl.pallas_call(
        functools.partial(join_kernel, main, rest),
        out_shape=(out, out),
        in_specs=[pl.BlockSpec(memory_space=pltpu.VMEM)] * 3,
        out_specs=(pl.BlockSpec(memory_space=pltpu.VMEM),) * 2,
        name="join",
    )(near, keep, give)


def split_pair(block):
    main, rest = parts_of(block.shape[1] * 2)
    first = jnp.concatenate([block[:, :main], block[:, 2 * main : 2 * main + rest]], axis=1)
    second = jnp.concatenate([block[:, main : 2 * main], block[:, 2 * main + rest :]], axis=1)
    return first, second


def join_pair(first, second):
    main, rest = parts_of(first.shape[1] * 4)
    return jnp.concatenate(
        [first[:, :main], second[:, :main], first[:, main:], second[:, main:]], axis=1
    )


def ordered(own, other, first):
    return jnp.where(first, jnp.stack([own, other]), jnp.stack([other, own]))


def halves(row):
    high = row.astype(BF16)
    return high, (row - high.astype(F32)).astype(BF16)


def with_rows(block, *rows):
    shape = (EXTRA, block.shape[1])
    which = lax.broadcasted_iota(jnp.int32, shape, 0)
    tail = jnp.zeros(shape, BF16)
    for k, half in enumerate([half for row in rows for half in halves(row)]):
        tail = jnp.where(which == k, half[None, :], tail)
    return jnp.concatenate([block.astype(BF16), tail], axis=0)


def row_of(packed_rows, k=0):
    at_row = packed_rows.shape[0] - EXTRA + 2 * k
    return packed_rows[at_row].astype(F32) + packed_rows[at_row + 1].astype(F32)


def block_of(packed_rows):
    return packed_rows[: packed_rows.shape[0] - EXTRA].astype(F32)


def derivatives(gate, up, back):
    hidden, pull = jax.vjp(lambda g, u: jax.nn.gelu(g, approximate=True) * u, gate, up)
    return pull(back)


def shards(tokens, hidden_grad, norm_gain, w_gate, w_up):
    rows, width = w_gate.shape
    group = tokens.shape[0]
    features = norm_gain.shape[0]
    own_rows = features // 16
    barrier = lax.optimization_barrier

    zh, x, core, tp, sec = (unsigned(lax.axis_index(a)) for a in (*DP, *COLS))
    steps = (1, 3, 2)
    far_zh, other_core = 1 - zh, 1 - core
    first_core = core == 0
    x_to = {by: (x + by) & 3 for by in range(4)}
    sec_to = {by: (sec + by) & 3 for by in range(4)}
    tp_to = {by: (tp + by) & 3 for by in range(4)}
    offset = (tp * 4 + sec) * own_rows
    tp_to, offset, hidden_grad = barrier((tp_to, offset, hidden_grad))

    own_t = tokens.T
    far_t = swapped(own_t, "zh")

    near_own, near_other = packed(0, w_gate, w_up, hidden_grad)
    hidden_grad, near_own = barrier((hidden_grad, near_own))
    away_own, away_other, backs = packed(1, w_gate, w_up, hidden_grad)
    near_other = swapped(near_other, "core")
    away_other, far_t = barrier((away_other, far_t))
    away_own, away_other = swapped(away_own, "zh"), swapped(away_other, "zh")

    near = ordered(near_own[:rows], near_other[:rows], first_core)
    near, own_t = barrier((near, own_t))
    near_got = [turned(near, "x", by) for by in steps]

    both = jnp.concatenate([own_t, far_t], axis=1)
    both, near_got[0], near_got[1] = barrier((both, near_got[0], near_got[1]))
    section_got = [turned(both, "sec", by) for by in steps]

    near_got[0], near_got[1], backs, late_first = barrier(
        (near_got[0], near_got[1], backs, first_core)
    )
    away_other = swapped(away_other, "core")
    backs = swapped(backs, "zh")
    away = ordered(away_own, away_other, late_first)
    late = {}
    away, late[0], late[1], late[2], late[3] = barrier((away, *(sec_to[by] for by in range(4))))
    away_got = [turned(away, "x", by) for by in steps]

    inputs = jnp.zeros((4, *both.shape), BF16)
    for by, piece in zip((0, 3, 1, 2), (both, *section_got)):
        inputs = put(inputs, piece, late[by])
    inputs = inputs.reshape(features, 2 * group)
    wide = inputs.astype(F32)
    inv_rms = lax.rsqrt(jnp.mean(wide * wide, axis=0) + EPS)
    normed = (wide * inv_rms * norm_gain[:, None]).astype(BF16)
    normed, away_got[0] = barrier((normed, away_got[0]))
    normed_other, away_got[2] = barrier((swapped(normed, "core"), away_got[2]))
    normed = jnp.concatenate([normed, normed_other], axis=1)

    backs, away_got[0], away_got[2] = barrier((backs, away_got[0], away_got[2]))
    back_other, away_got[1] = barrier((swapped(backs[1], "core"), away_got[1]))
    full = jnp.zeros((2, 4, 2, rows, width // 2), BF16)
    for pieces, place in (((near, *near_got), zh), ((away, *away_got), far_zh)):
        for by, piece in zip((0, 3, 1, 2), pieces):
            full = put(full, piece, place, x_to[by])
    full = full.reshape(features, -1)
    back = jnp.concatenate(
        [
            half
            for block in (near_own[rows:], backs[0], near_other[rows:], back_other)
            for half in split_pair(block)
        ],
        axis=0,
    )

    product = lax.dot_general(
        normed, full, (((0,), (0,)), ((), ())), preferred_element_type=F32
    )
    gate, up = split_pair(product)
    d_gate, d_up = derivatives(gate, up, back.astype(F32))
    d_gate, d_up = d_gate.astype(BF16), d_up.astype(BF16)
    row_part = jnp.sum(d_gate.astype(F32) * gate + d_up.astype(F32) * up, axis=1)
    d_both = join_pair(d_gate, d_up)

    def d_normed(d):
        return lax.dot_general(full, d, (((1,), (1,)), ((), ())), preferred_element_type=F32)

    by_rows = normed.reshape(2, 4, 2 * rows, 4 * group)

    def part(zplace, xplace):
        return jnp.dot(as_block(by_rows, zplace, xplace), d_both, preferred_element_type=F32)

    away_parts = [part(far_zh, x_to[by]).astype(BF16) for by in steps]
    near_parts = [part(zh, x_to[by]).astype(BF16) for by in steps]
    away_got = [turned(away_parts[k], "x", steps[k]) for k in (0, 1)]

    got = swapped(d_normed(d_both[2 * group :]).astype(BF16), "core")
    row = row_part[: 2 * group] + swapped(row_part[2 * group :], "core")
    mine = d_normed(d_both[: 2 * group]) + got.astype(F32)
    mine = mine.reshape(4, 4, own_rows, 2 * group)

    def section(index):
        zero = jnp.uint32(0)
        block = lax.dynamic_slice(
            mine, (zero, index, zero, zero), (4, 1, own_rows, 2 * group)
        )
        return block.reshape(4 * own_rows, 2 * group)

    sends = [with_rows(section(sec_to[by]), row) for by in steps]
    *away_got, away_parts[2], sends[0], sends[1], sends[2] = barrier(
        (*away_got, away_parts[2], *sends)
    )
    away_got.append(turned(away_parts[2], "x", 2))
    got = [turned(s, "sec", by) for s, by in zip(sends, steps)]
    away_got[2], *near_parts = barrier((away_got[2], *near_parts))
    near_got = [turned(p, "x", by) for p, by in zip(near_parts, steps)]
    g_away = part(far_zh, x) + sum(g.astype(F32) for g in away_got)
    g_away = g_away.astype(BF16).reshape(2, rows, -1)
    late = {}
    g_away, late[1], late[3], late[2] = barrier((g_away, *(tp_to[by] for by in steps)))
    away_keep = swapped(as_block(g_away, core), "zh")
    away_give = swapped(as_block(g_away, other_core), "zh")

    total = section(sec) + sum(block_of(g) for g in got)
    row = row + sum(row_of(g) for g in got)
    mine = total.reshape(4, own_rows, 2 * group)
    sends = [with_rows(as_block(mine, late[by]), row) for by in steps]
    got = [turned(s, "tp", by) for s, by in zip(sends, steps)]
    total = as_block(mine, tp) + sum(block_of(g) for g in got)
    row = row + sum(row_of(g) for g in got)

    own_inputs = lax.dynamic_slice(inputs, (offset, jnp.uint32(0)), (own_rows, 2 * group))
    own_inputs = own_inputs.astype(F32)
    own_gain = lax.dynamic_slice(norm_gain, (offset,), (own_rows,))[:, None]
    gain_part = jnp.sum(total * own_inputs * inv_rms, axis=1)
    gain_rows = jnp.pad(gain_part, (0, 2 * group - own_rows)).reshape(2, group)
    send = with_rows(total[:, group:], row[group:], gain_rows[0], gain_rows[1])
    send, near_got[0], near_got[1], late_zh = barrier((send, near_got[0], near_got[1], zh))
    got = swapped(send, "zh")
    g_near = part(late_zh, x) + sum(g.astype(F32) for g in near_got)
    g_near = g_near.astype(BF16).reshape(2, rows, -1)
    give = swapped(jnp.stack([as_block(g_near, other_core), away_give]), "core")
    grad_gain = gain_part + jnp.concatenate([row_of(got, 1), row_of(got, 2)])[:own_rows]
    grad_gain = grad_gain + swapped(grad_gain, "core")
    grad_gain = grad_gain + sum(turned(grad_gain, "x", by) for by in steps)
    d_own, row_sum = total[:, :group] + block_of(got), row[:group] + row_of(got)
    inv = inv_rms[:group]
    own_inputs = own_inputs[:, :group]
    grad_tokens = inv * own_gain * d_own - own_inputs * (inv**2 * row_sum / features)
    grad_gate, grad_up = joined(g_near, away_keep, give)
    return grad_tokens.T.astype(BF16), grad_gain, grad_gate, grad_up


def solution(mesh):
    split = Mesh(
        mesh.devices.reshape(2, 4, 2, mesh.shape["tp"], mesh.shape["section"]),
        (*DP, *COLS),
    )
    weights = P(DP, COLS)
    return jax.shard_map(
        shards,
        mesh=split,
        in_specs=(P(DP, "sec"), weights, P(), weights, weights),
        out_specs=(weights, P(COLS), weights, weights),
        check_vma=False,
    )
```

```python
import functools

import jax
import jax.numpy as jnp
from jax import lax
from jax.experimental import pallas as pl
from jax.experimental.pallas import tpu as pltpu
from jax.sharding import Mesh
from jax.sharding import PartitionSpec as P

DP = ("zh", "x", "core")
COLS = ("tp", "sec")
EPS = 1e-06
LANES = 128
EXTRA = 16
F32 = jnp.float32
BF16 = jnp.bfloat16
SDS = jax.ShapeDtypeStruct


def turned(array, axis, by):
    n = lax.axis_size(axis)
    return lax.ppermute(array, axis, [(i, (i + by) % n) for i in range(n)])


def swapped(array, axis):
    return turned(array, axis, 1)


def unsigned(index):
    return index.astype(jnp.uint32)


def as_block(array, *lead):
    n = len(lead)
    zeros = [jnp.uint32(0)] * (array.ndim - n)
    part = lax.dynamic_slice(array, (*lead, *zeros), (*([1] * n), *array.shape[n:]))
    return part.reshape(array.shape[n:])


def put(array, part, *lead):
    zeros = [jnp.uint32(0)] * (array.ndim - len(lead))
    part = part.reshape(*([1] * len(lead)), *array.shape[len(lead) :])
    return lax.dynamic_update_slice(array, part, (*lead, *zeros))


def parts_of(width):
    main = width // LANES // 4 * LANES
    rest = width // 4 - main
    return main, rest


def pack_kernel(main, rest, aways, gate_ref, up_ref, back_ref, *outs):
    half = back_ref.shape[0] // 2
    zh, core = lax.axis_index("zh"), lax.axis_index("core")
    rows = gate_ref.shape[0]
    if aways:
        weights, backs = outs[:2], [outs[2].at[0], outs[2].at[1]]
    else:
        weights = [out.at[pl.ds(0, rows)] for out in outs]
        backs = [out.at[pl.ds(rows, half)] for out in outs]
    sources = (
        (weights, gate_ref, up_ref),
        (backs, back_ref.at[pl.ds(0, half)], back_ref.at[pl.ds(half, half)]),
    )
    for other in range(2):
        q = (zh ^ aways) * 2 + (core ^ other)
        wide = pl.ds(pl.multiple_of(q * main, LANES), main)
        for targets, first, second in sources:
            out = targets[other]
            out[:, pl.ds(0, main)] = first[:, wide]
            out[:, pl.ds(main, main)] = second[:, wide]
            thin = []
            for ref in (first, second):
                tail = ref[:, pl.ds(4 * main, 4 * rest)]
                turn = pltpu.roll(tail.astype(F32), ((4 - q) & 3) * rest, 1)
                thin.append(turn[:, :rest].astype(BF16))
            out[:, pl.ds(2 * main, 2 * rest)] = jnp.concatenate(thin, axis=1)


def packed(aways, w_gate, w_up, hidden_grad):
    rows, width = w_gate.shape
    main, rest = parts_of(width)
    half = hidden_grad.shape[0] // 2
    if aways:
        outs = [(rows, width // 2), (rows, width // 2), (2, half, width // 2)]
    else:
        outs = [(rows + half, width // 2)] * 2
    return pl.pallas_call(
        functools.partial(pack_kernel, main, rest, aways),
        out_shape=[pltpu.VMEM(shape, BF16) for shape in outs],
        in_specs=[pl.BlockSpec(memory_space=pltpu.VMEM)] * 3,
        out_specs=[pl.BlockSpec(memory_space=pltpu.VMEM)] * len(outs),
        name="pack",
    )(w_gate, w_up, hidden_grad)


def join_kernel(main, rest, near_ref, keep_ref, give_ref, gate_ref, up_ref):
    zh, core = lax.axis_index("zh"), lax.axis_index("core")
    tails = [[None] * 4, [None] * 4]
    for aways in range(2):
        for other in range(2):
            ref = give_ref.at[aways] if other else keep_ref if aways else near_ref.at[core]
            q = (zh ^ aways) * 2 + (core ^ other)
            wide = pl.ds(pl.multiple_of(q * main, LANES), main)
            gate_ref[:, wide] = ref[:, pl.ds(0, main)]
            up_ref[:, wide] = ref[:, pl.ds(main, main)]
            tail = ref[:, pl.ds(2 * main, 2 * rest)]
            for i in range(2):
                thin = tail[:, i * rest : (i + 1) * rest]
                for k in range(4):
                    old = tails[i][k]
                    tails[i][k] = thin if old is None else jnp.where(q == k, thin, old)
    gate_ref[:, pl.ds(4 * main, 4 * rest)] = jnp.concatenate(tails[0], axis=1)
    up_ref[:, pl.ds(4 * main, 4 * rest)] = jnp.concatenate(tails[1], axis=1)


def joined(near, keep, give):
    rows, half = keep.shape
    main, rest = parts_of(half * 2)
    out = SDS((rows, half * 2), BF16)
    return pl.pallas_call(
        functools.partial(join_kernel, main, rest),
        out_shape=(out, out),
        in_specs=[pl.BlockSpec(memory_space=pltpu.VMEM)] * 3,
        out_specs=(pl.BlockSpec(memory_space=pltpu.VMEM),) * 2,
        name="join",
    )(near, keep, give)


def split_pair(block):
    main, rest = parts_of(block.shape[1] * 2)
    first = jnp.concatenate([block[:, :main], block[:, 2 * main : 2 * main + rest]], axis=1)
    second = jnp.concatenate([block[:, main : 2 * main], block[:, 2 * main + rest :]], axis=1)
    return first, second


def join_pair(first, second):
    main, rest = parts_of(first.shape[1] * 4)
    return jnp.concatenate(
        [first[:, :main], second[:, :main], first[:, main:], second[:, main:]], axis=1
    )


def ordered(own, other, first):
    return jnp.where(first, jnp.stack([own, other]), jnp.stack([other, own]))


def halves(row):
    high = row.astype(BF16)
    return high, (row - high.astype(F32)).astype(BF16)


def with_rows(block, *rows):
    shape = (EXTRA, block.shape[1])
    which = lax.broadcasted_iota(jnp.int32, shape, 0)
    tail = jnp.zeros(shape, BF16)
    for k, half in enumerate([half for row in rows for half in halves(row)]):
        tail = jnp.where(which == k, half[None, :], tail)
    return jnp.concatenate([block.astype(BF16), tail], axis=0)


def row_of(packed_rows, k=0):
    at_row = packed_rows.shape[0] - EXTRA + 2 * k
    return packed_rows[at_row].astype(F32) + packed_rows[at_row + 1].astype(F32)


def block_of(packed_rows):
    return packed_rows[: packed_rows.shape[0] - EXTRA].astype(F32)


def derivatives(gate, up, back):
    hidden, pull = jax.vjp(lambda g, u: jax.nn.gelu(g, approximate=True) * u, gate, up)
    return pull(back)


def shards(tokens, hidden_grad, norm_gain, w_gate, w_up):
    rows, width = w_gate.shape
    group = tokens.shape[0]
    features = norm_gain.shape[0]
    own_rows = features // 16
    barrier = lax.optimization_barrier

    zh, x, core, tp, sec = (unsigned(lax.axis_index(a)) for a in (*DP, *COLS))
    steps = (1, 3, 2)
    far_zh, other_core = 1 - zh, 1 - core
    first_core = core == 0
    x_to = {by: (x + by) & 3 for by in range(4)}
    sec_to = {by: (sec + by) & 3 for by in range(4)}
    tp_to = {by: (tp + by) & 3 for by in range(4)}
    offset = (tp * 4 + sec) * own_rows
    tp_to, offset, hidden_grad = barrier((tp_to, offset, hidden_grad))

    own_t = tokens.T
    far_t = swapped(own_t, "zh")

    near_own, near_other = packed(0, w_gate, w_up, hidden_grad)
    hidden_grad, near_own = barrier((hidden_grad, near_own))
    away_own, away_other, backs = packed(1, w_gate, w_up, hidden_grad)
    near_other = swapped(near_other, "core")
    away_other, far_t = barrier((away_other, far_t))
    away_own, away_other = swapped(away_own, "zh"), swapped(away_other, "zh")

    near = ordered(near_own[:rows], near_other[:rows], first_core)
    near, own_t = barrier((near, own_t))
    near_got = [turned(near, "x", by) for by in steps]

    both = jnp.concatenate([own_t, far_t], axis=1)
    both, near_got[0], near_got[1] = barrier((both, near_got[0], near_got[1]))
    section_got = [turned(both, "sec", by) for by in steps]

    near_got[0], near_got[1], backs, late_first = barrier(
        (near_got[0], near_got[1], backs, first_core)
    )
    away_other = swapped(away_other, "core")
    backs = swapped(backs, "zh")
    away = ordered(away_own, away_other, late_first)
    late = {}
    away, late[0], late[1], late[2], late[3] = barrier((away, *(sec_to[by] for by in range(4))))
    away_got = [turned(away, "x", by) for by in steps]

    inputs = jnp.zeros((4, *both.shape), BF16)
    for by, piece in zip((0, 3, 1, 2), (both, *section_got)):
        inputs = put(inputs, piece, late[by])
    inputs = inputs.reshape(features, 2 * group)
    wide = inputs.astype(F32)
    inv_rms = lax.rsqrt(jnp.mean(wide * wide, axis=0) + EPS)
    normed = (wide * inv_rms * norm_gain[:, None]).astype(BF16)
    normed, away_got[0] = barrier((normed, away_got[0]))
    normed_other, away_got[2] = barrier((swapped(normed, "core"), away_got[2]))
    normed = jnp.concatenate([normed, normed_other], axis=1)

    backs, *away_got = barrier((backs, *away_got))
    full = jnp.zeros((2, 4, 2, rows, width // 2), BF16)
    for pieces, place in (((near, *near_got), zh), ((away, *away_got), far_zh)):
        for by, piece in zip((0, 3, 1, 2), pieces):
            full = put(full, piece, place, x_to[by])
    full = full.reshape(features, -1)
    back = jnp.concatenate(
        [
            half
            for block in (near_own[rows:], backs[0], near_other[rows:], swapped(backs[1], "core"))
            for half in split_pair(block)
        ],
        axis=0,
    )

    product = lax.dot_general(
        normed, full, (((0,), (0,)), ((), ())), preferred_element_type=F32
    )
    gate, up = split_pair(product)
    d_gate, d_up = derivatives(gate, up, back.astype(F32))
    d_gate, d_up = d_gate.astype(BF16), d_up.astype(BF16)
    row_part = jnp.sum(d_gate.astype(F32) * gate + d_up.astype(F32) * up, axis=1)
    d_both = join_pair(d_gate, d_up)

    def d_normed(d):
        return lax.dot_general(full, d, (((1,), (1,)), ((), ())), preferred_element_type=F32)

    by_rows = normed.reshape(2, 4, 2 * rows, 4 * group)

    def part(zplace, xplace):
        return jnp.dot(as_block(by_rows, zplace, xplace), d_both, preferred_element_type=F32)

    away_parts = [part(far_zh, x_to[by]).astype(BF16) for by in steps]
    away_got = [turned(away_parts[k], "x", steps[k]) for k in (0, 1)]

    got = swapped(d_normed(d_both[2 * group :]).astype(BF16), "core")
    got, near_zh = barrier((got, zh))
    near_parts = [part(near_zh, x_to[by]).astype(BF16) for by in steps]
    row = row_part[: 2 * group] + swapped(row_part[2 * group :], "core")
    mine = d_normed(d_both[: 2 * group]) + got.astype(F32)
    mine = mine.reshape(4, 4, own_rows, 2 * group)

    def section(index):
        zero = jnp.uint32(0)
        block = lax.dynamic_slice(
            mine, (zero, index, zero, zero), (4, 1, own_rows, 2 * group)
        )
        return block.reshape(4 * own_rows, 2 * group)

    sends = [with_rows(section(sec_to[by]), row) for by in steps]
    *away_got, away_parts[2], sends[0], sends[1], sends[2] = barrier(
        (*away_got, away_parts[2], *sends)
    )
    away_got.append(turned(away_parts[2], "x", 2))
    got = [turned(s, "sec", by) for s, by in zip(sends, steps)]
    away_got[2], *near_parts = barrier((away_got[2], *near_parts))
    near_got = [turned(p, "x", by) for p, by in zip(near_parts, steps)]
    g_away = part(far_zh, x) + sum(g.astype(F32) for g in away_got)
    g_away = g_away.astype(BF16).reshape(2, rows, -1)
    late = {}
    g_away, late[1], late[3], late[2] = barrier((g_away, *(tp_to[by] for by in steps)))
    away_keep = swapped(as_block(g_away, core), "zh")
    away_give = swapped(as_block(g_away, other_core), "zh")

    total = section(sec) + sum(block_of(g) for g in got)
    row = row + sum(row_of(g) for g in got)
    mine = total.reshape(4, own_rows, 2 * group)
    sends = [with_rows(as_block(mine, late[by]), row) for by in steps]
    got = [turned(s, "tp", by) for s, by in zip(sends, steps)]
    total = as_block(mine, tp) + sum(block_of(g) for g in got)
    row = row + sum(row_of(g) for g in got)

    own_inputs = lax.dynamic_slice(inputs, (offset, jnp.uint32(0)), (own_rows, 2 * group))
    own_inputs = own_inputs.astype(F32)
    own_gain = lax.dynamic_slice(norm_gain, (offset,), (own_rows,))[:, None]
    gain_part = jnp.sum(total * own_inputs * inv_rms, axis=1)
    gain_rows = jnp.pad(gain_part, (0, 2 * group - own_rows)).reshape(2, group)
    send = with_rows(total[:, group:], row[group:], gain_rows[0], gain_rows[1])
    send, near_got[0], near_got[1], late_zh = barrier((send, near_got[0], near_got[1], zh))
    got = swapped(send, "zh")
    g_near = part(late_zh, x) + sum(g.astype(F32) for g in near_got)
    g_near = g_near.astype(BF16).reshape(2, rows, -1)
    give = swapped(jnp.stack([as_block(g_near, other_core), away_give]), "core")
    grad_gain = gain_part + jnp.concatenate([row_of(got, 1), row_of(got, 2)])[:own_rows]
    grad_gain = grad_gain + swapped(grad_gain, "core")
    grad_gain = grad_gain + sum(turned(grad_gain, "x", by) for by in steps)
    d_own, row_sum = total[:, :group] + block_of(got), row[:group] + row_of(got)
    inv = inv_rms[:group]
    own_inputs = own_inputs[:, :group]
    grad_tokens = inv * own_gain * d_own - own_inputs * (inv**2 * row_sum / features)
    grad_gate, grad_up = joined(g_near, away_keep, give)
    return grad_tokens.T.astype(BF16), grad_gain, grad_gate, grad_up


def solution(mesh):
    split = Mesh(
        mesh.devices.reshape(2, 4, 2, mesh.shape["tp"], mesh.shape["section"]),
        (*DP, *COLS),
    )
    weights = P(DP, COLS)
    return jax.shard_map(
        shards,
        mesh=split,
        in_specs=(P(DP, "sec"), weights, P(), weights, weights),
        out_specs=(weights, P(COLS), weights, weights),
        check_vma=False,
    )
```
